256 devices in a mesh: domain: 16 (over z, y_lo), band: 16 (over x, y_hi, core).
Axes of the slice: x: 4, y: 4 (y_hi: 2, y_lo: 2; y = y_hi * 2 + y_lo), z: 8, core: 2. Of those that a mesh axis runs over, the one named last changes fastest.
Arguments:
- states: float32 [19584, 2048], P('domain', 'band'), may hold values from -6 to 6
- potential: float32 [19584], P('domain'), may hold values from -1 to 1
- node_mass: float32 [19584], P('domain'), may hold values from 0.3 to 3
- cell_matrix: bfloat16 [729, 729], replicated, as said below
- connectivity: int32 [32, 729], P('domain'), may hold values from 0 to 1376, as said below
- face_rows: int32 [16, 153], P('domain'), may hold values from 0 to 1223, as said below
Outputs:
- subspace: float32 [19584, 2048], P('domain', 'band')
The draws below stay inside these ranges and needn't reach their ends.
Inputs may be any that keep to these rules, and one draw needn't show every extreme that they name: `connectivity`: row c lists, for cell c of its slab, the storage rows of the cell's 729 nodes, all different. A value v of 1224 or more names the node held by the upper neighbouring slab in row face_rows[s + 1, v - 1224]. `face_rows`: row s lists the storage rows of slab s's lower face nodes, all different; the storage rows of a slab are a permutation of its 1224 nodes. `cell_matrix`: Symmetric; its diagonal lies between 0.8 and 1.2.
All inputs are finite; a program needn't handle non-finite values.
Results may differ from the reference program's by a relative error of at most 0.0028.
Values may be sent and summed in bfloat16 or wider, within the bound.
A program may use at most 64 MiB of HBM per device.

```python
import math
import jax
import jax.numpy as jnp
from jax import lax

EDGE = 9
CELL_NODES = 729
CX = 1
CY = 2
CZ = 1
PANEL = 256
DEGREE = 6
CELLS_DEV = 2
NXN = 9
NYN = 17
FACE = 153
OWNED = 1224
NSLAB = 16
NODES = 19584
STATES = 2048


def place_value(order, value, position):
    index = jnp.arange(OWNED, dtype=jnp.int32)
    at_slot = order[position]
    return jnp.where(index == position, value, jnp.where(order == value, at_slot, order)).astype(jnp.int32)


def one_order(subkey):
    order = jax.random.permutation(subkey, OWNED).astype(jnp.int32)
    order = place_value(order, OWNED - 1, 0)
    return place_value(order, 0, 1)


def storage_order(key):
    subkeys = jax.random.split(jax.random.fold_in(key, 11), NSLAB)
    return jax.vmap(one_order)(subkeys).astype(jnp.int32)


def draw_cell_matrix(key, part):
    first_key, second_key = jax.random.split(jax.random.fold_in(key, 5))
    noise = jax.random.normal(first_key, (CELL_NODES, CELL_NODES), jnp.float32)
    diagonal = jax.random.uniform(second_key, (CELL_NODES,), jnp.float32, 0.8, 1.2)
    coupling = (noise + noise.T) * (0.3 / jnp.sqrt(2.0 * CELL_NODES))
    coupling = coupling * (1.0 - jnp.eye(CELL_NODES, dtype=jnp.float32))
    return (coupling + jnp.diag(diagonal)).astype(jnp.bfloat16)


def draw_connectivity(key, part):
    orders = storage_order(key)
    spacing = EDGE - 1
    cell_index = jnp.arange(CELLS_DEV, dtype=jnp.int32)
    cell_first = cell_index % CX
    cell_second = cell_index // CX % CY
    cell_third = cell_index // (CX * CY)
    node_index = jnp.arange(CELL_NODES, dtype=jnp.int32)
    node_first = node_index % EDGE
    node_second = node_index // EDGE % EDGE
    node_third = node_index // (EDGE * EDGE)
    grid_first = cell_first[:, None] * spacing + node_first[None, :]
    grid_second = cell_second[:, None] * spacing + node_second[None, :]
    grid_third = cell_third[:, None] * spacing + node_third[None, :]
    on_top = grid_third == spacing * CZ
    grid_index = jnp.where(on_top, 0, (grid_third * NYN + grid_second) * NXN + grid_first)
    face_index = grid_second * NXN + grid_first

    def one_slab(order):
        return jnp.where(on_top, OWNED + face_index, order[grid_index])
    return jax.vmap(one_slab)(orders).reshape(NSLAB * CELLS_DEV, CELL_NODES).astype(jnp.int32)


def draw_face_rows(key, part):
    orders = storage_order(key)
    return orders[:, :FACE].astype(jnp.int32)


def block_scale(key, extent, cuts, least, high):
    level = 1.0
    for axis_at, parts in cuts:
        heights = jax.random.uniform(jax.random.fold_in(jax.random.fold_in(key, 6), axis_at), (parts,), jnp.float32, least / len(cuts), high / len(cuts))
        level = level * jnp.repeat(jnp.exp(heights), extent[axis_at] // parts).reshape((-1,) + (1,) * (len(extent) - 1 - axis_at))
    return level


def gaussian(key, shape, scale, reach, cuts=(), held_as=jnp.bfloat16):
    factor_of = block_scale(key, shape, cuts, -0.22, 0.18) if cuts else 1.0
    drawn = jax.random.normal(key, shape, jnp.float32) * scale * factor_of
    return jnp.minimum(jnp.maximum(drawn, -reach), reach).astype(held_as)


def setup_inputs(seed: int = 0) -> dict:
    key_of = jax.random.split(jax.random.key(seed), 7)
    return {
        "states": gaussian(key_of[0], (NODES, STATES), 1.0, 6.0, ((0, 16), (1, 16)), jnp.float32),
        "potential": jnp.clip(jax.random.uniform(key_of[1], (NODES,), jnp.float32, -1.0, 1.0) * block_scale(key_of[1], (NODES,), ((0, 16),), -0.4, 0.0), -1.0, 1.0),
        "node_mass": jnp.clip(jnp.exp(math.log(3.0) - 2.3025851 * jax.random.uniform(key_of[2], (NODES,), jnp.float32) ** block_scale(key_of[2], (NODES,), ((0, 16),), -0.2, 0.2)), 0.3, 3.0),
        "cell_matrix": draw_cell_matrix(jax.random.fold_in(key_of[6], 71), 0),
        "connectivity": draw_connectivity(jax.random.fold_in(key_of[6], 71), 0),
        "face_rows": draw_face_rows(jax.random.fold_in(key_of[6], 71), 0),
    }


centre = 9.0
half_width = 8.0
highest = lax.Precision.HIGHEST

def contract(left_side, right_side):
    return jnp.einsum('nk,nj->kj', left_side.astype(jnp.float32), right_side.astype(jnp.float32), precision=highest, preferred_element_type=jnp.float32)

def product(left_side, right_side):
    return jnp.dot(left_side.astype(jnp.float32), right_side.astype(jnp.float32), precision=highest, preferred_element_type=jnp.float32)

def global_rows(connectivity, face_rows):
    slab_of = (jnp.arange(NSLAB * CELLS_DEV) // CELLS_DEV).astype(jnp.int32)[:, None]
    upper_slab = jnp.minimum(slab_of[:, 0] + 1, NSLAB - 1).astype(jnp.int32)
    upper_faces = face_rows[upper_slab]
    ghost_slot = jnp.clip(connectivity - OWNED, 0, FACE - 1).astype(jnp.int32)
    ghost_rows = jnp.take_along_axis(upper_faces, ghost_slot, axis=1)
    inside_rows = slab_of * OWNED + connectivity
    above_rows = jnp.where(slab_of < NSLAB - 1, (slab_of + 1) * OWNED + ghost_rows, NODES)
    return jnp.where(connectivity < OWNED, inside_rows, above_rows).astype(jnp.int32)

def apply_operator(current, cell_matrix, potential, node_rows):
    rounded = jnp.concatenate([current.astype(jnp.bfloat16), jnp.zeros((1, current.shape[1]), jnp.bfloat16)], axis=0)

    def one_cell(number, summed):
        cell_nodes = node_rows[number]
        local_terms = jnp.dot(cell_matrix.astype(jnp.float32), rounded[cell_nodes].astype(jnp.float32), preferred_element_type=jnp.float32)
        return summed.at[cell_nodes].add(local_terms)
    summed = lax.fori_loop(0, node_rows.shape[0], one_cell, jnp.zeros((NODES + 1, current.shape[1]), jnp.float32))
    return summed[:NODES] + potential[:, None] * current

def orthonormal(panel_cols, targets, weights):
    gram_matrix = contract(panel_cols * weights[:, None], panel_cols)
    factor = jnp.linalg.cholesky(gram_matrix)
    basis_cols = jax.scipy.linalg.solve_triangular(factor, panel_cols.T, lower=True).T
    coefficients = contract(basis_cols * weights[:, None], targets)
    return (basis_cols, targets - product(basis_cols, coefficients))

def reference(states, potential, node_mass, cell_matrix, connectivity, face_rows):
    node_rows = global_rows(connectivity, face_rows)
    previous = states
    current = (apply_operator(states, cell_matrix, potential, node_rows) - centre * states) / half_width
    for repeat in range(DEGREE - 1):
        following = 2.0 * (apply_operator(current, cell_matrix, potential, node_rows) - centre * current) / half_width - previous
        previous, current = (current, following)
    weights = node_mass / NODES
    basis_one, rest_one = orthonormal(current[:, :PANEL], current[:, PANEL:], weights)
    basis_two, rest_two = orthonormal(rest_one[:, :PANEL], rest_one[:, PANEL:], weights)
    return jnp.concatenate([basis_one, basis_two, rest_two], axis=1)
```

```python
import functools
import jax
import jax.numpy as jnp
from jax import lax
from jax.experimental import pallas as pl
from jax.experimental.pallas import tpu as pltpu
from jax.sharding import PartitionSpec as P

f32 = jnp.float32
bf16 = jnp.bfloat16
i32 = jnp.int32
OWNED = 1224
ROWS = 1280
CELL = 729
CP = 768
CS = 1536
FACE = 153
FP = 160
COLS = 128
DEGREE = 6
ND = 16
MESHID = pl.DeviceIdType.MESH
VM = pl.BlockSpec(memory_space=pltpu.VMEM)


def dot(a, b):
    return jnp.dot(a, b, preferred_element_type=f32)


def split2(x):
    hi = x.astype(bf16)
    return hi, (x - hi.astype(f32)).astype(bf16)


def split3(x):
    hi = x.astype(bf16)
    rest = x - hi.astype(f32)
    mid = rest.astype(bf16)
    return hi, mid, (rest - mid.astype(f32)).astype(bf16)


def lanes(shape, base=0):
    return lax.broadcasted_iota(i32, shape, 1) + base


def subs(shape, base=0):
    return lax.broadcasted_iota(i32, shape, 0) + base


def onehot(mask):
    return jnp.where(mask, 1.0, 0.0).astype(bf16)


def filter_kernel(v_ref, pot_ref, mat_ref, conn_ref, face_ref, out_ref,
                  crow, frow, connb, faceb, potb, kp, amat, afac, bmat, gt, ft, gsel, v3, potc, potf, msk,
                  cnt, ws, wb, wf, ybuf, rb, send, recv, vsend, vrecv, ssem, rsem, vsem):
    d = lax.axis_index("domain")
    vrecv[...] = jnp.zeros(vrecv.shape, f32)
    recv[...] = jnp.zeros(recv.shape, f32)
    barrier = pltpu.get_barrier_semaphore()

    for k in (1, ND - 1):
        pl.semaphore_signal(barrier, inc=1, device_id={"domain": lax.rem(d + k, ND)}, device_id_type=MESHID)

    crow[...] = jnp.full(crow.shape, -1.0, f32)
    crow[0:1, 0:CELL] = conn_ref[0:1, :].astype(f32)
    crow[0:1, CP:CP + CELL] = conn_ref[1:2, :].astype(f32)
    frow[...] = jnp.full(frow.shape, -2.0, f32)
    frow[0:1, 0:FACE] = face_ref[0:1, :].astype(f32)
    for t in range(CS // 128):
        row = crow[0:1, 128 * t:128 * t + 128]
        connb[128 * t:128 * t + 128, :] = jnp.broadcast_to(row, (128, 128)).T.astype(i32)
    for t in range(2):
        row = frow[0:1, 128 * t:128 * t + 128]
        faceb[128 * t:128 * t + 128, :] = jnp.broadcast_to(row, (128, 128)).T.astype(i32)
    potb[1152:1280, :] = jnp.zeros((128, 128), f32)
    v3[1216:ROWS, :] = jnp.zeros((ROWS - 1216, 640), bf16)
    for t in range(9):
        row = pot_ref[0:1, 128 * t:128 * t + 128]
        potb[128 * t:128 * t + 128, :] = jnp.broadcast_to(row, (128, 128)).T
    last = jnp.broadcast_to(pot_ref[0:1, OWNED - 128:OWNED], (128, 128)).T
    potb[OWNED - 128:OWNED, :] = last
    hi, mid, lo = split3(v_ref[...])
    v3[0:OWNED, 0:128] = hi
    v3[0:OWNED, 128:256] = mid
    v3[0:OWNED, 256:384] = lo
    hi, lo = split2(potb[0:OWNED, :])
    v3[0:OWNED, 384:512] = hi
    v3[0:OWNED, 512:640] = lo

    fsel = onehot(jnp.tile(faceb[0:FP, :], (1, ROWS // 128)) == lanes((FP, ROWS)))
    fv = dot(fsel, v3[...])
    vface = fv[:, 0:128] + fv[:, 128:256] + fv[:, 256:384]
    potf[...] = fv[:, 384:512] + fv[:, 512:640]
    wf[0] = vface
    wf[1] = jnp.zeros((FP, COLS), f32)
    vsend[...] = vface
    ws[1] = jnp.zeros((CS, COLS), f32)

    pl.semaphore_wait(barrier, 2)

    def vcopy(dst):
        return pltpu.make_async_remote_copy(
            src_ref=vsend, dst_ref=vrecv.at[pl.ds(0, FP), :], send_sem=vsem.at[0], recv_sem=vsem.at[1],
            device_id={"domain": dst}, device_id_type=MESHID)

    @pl.when(d > 0)
    def _():
        vcopy(d - 1).start()

    kp[...] = jnp.zeros(kp.shape, bf16)
    kp[0:CELL, 0:CELL] = mat_ref[...]
    km = kp[...]
    amat[0:CP, 0:CP] = km
    amat[CP:CS, CP:CS] = km
    e01 = onehot(jnp.tile(connb[0:CP, :], (1, CP // 128)) == crow[0:1, CP:CS].astype(i32))
    e01 = jnp.where(jnp.tile(connb[0:CP, :], (1, CP // 128)) >= 0, e01, jnp.zeros_like(e01))
    amat[0:CP, CP:CS] = dot(e01, km).astype(bf16)
    e10 = onehot(jnp.tile(connb[CP:CS, :], (1, CP // 128)) == crow[0:1, 0:CP].astype(i32))
    e10 = jnp.where(jnp.tile(connb[CP:CS, :], (1, CP // 128)) >= 0, e10, jnp.zeros_like(e10))
    amat[CP:CS, 0:CP] = dot(e10, km).astype(bf16)
    ci = crow[0:1, :].astype(i32)
    tup = onehot((subs((FP, CS), OWNED) == ci))
    tlo = onehot(jnp.tile(faceb[0:FP, :], (1, CS // 128)) == ci)
    for c in range(2):
        cols = slice(CP * c, CP * c + CP)
        afac[0:FP, cols] = dot(tup[:, cols], km).astype(bf16)
        afac[FP:2 * FP, cols] = dot(tlo[:, cols], km).astype(bf16)
    fi = frow[0:1, :].astype(i32)
    cb2 = jnp.tile(connb[...], (1, 2))
    bmat[:, 0:256] = onehot(cb2 == fi)
    bmat[:, 256:512] = onehot(cb2 == lanes((CS, 256), OWNED))
    for t in range(ROWS // 128):
        gt[128 * t:128 * t + 128, :] = onehot(subs((128, CS), 128 * t) == ci)
        ft[128 * t:128 * t + 128, :] = onehot(subs((128, 256), 128 * t) == fi)
        gsel[:, 128 * t:128 * t + 128] = onehot(connb[...] == lanes((CS, 128), 128 * t))
    cv = dot(gsel[...], v3[...])
    ws[0] = cv[:, 0:128] + cv[:, 128:256] + cv[:, 256:384]
    potc[...] = cv[:, 384:512] + cv[:, 512:640]
    msk[...] = jnp.where((connb[...] >= OWNED) & (d == ND - 1), 0.0, 1.0)
    cnt[...] = dot(gt[...], jnp.ones((CS, COLS), bf16)) + dot(ft[...], jnp.ones((256, COLS), bf16))

    @pl.when(d < ND - 1)
    def _():
        vcopy(d).wait_recv()

    hi, mid, lo = split3(vrecv[...])
    gv = dot(bmat[:, 256:512], jnp.concatenate([hi, mid, lo], axis=1))
    first = ws[0] + (gv[:, 0:128] + gv[:, 128:256] + gv[:, 256:384])
    ws[0] = first
    wb[...] = first.astype(bf16)

    def up(t, dst):
        return pltpu.make_async_remote_copy(
            src_ref=send.at[t, 0], dst_ref=recv.at[t, pl.ds(0, FP), :], send_sem=ssem.at[t, 0], recv_sem=rsem.at[t, 0],
            device_id={"domain": dst}, device_id_type=MESHID)

    def down(t, dst):
        return pltpu.make_async_remote_copy(
            src_ref=send.at[t, 1], dst_ref=recv.at[t, pl.ds(256, FP), :], send_sem=ssem.at[t, 1], recv_sem=rsem.at[t, 1],
            device_id={"domain": dst}, device_id_type=MESHID)

    def step(t, carry):
        now, then = lax.rem(t, 2), lax.rem(t + 1, 2)
        coef = jnp.where(t == 0, 0.125, 0.25).astype(f32)
        keep = jnp.where(t == 0, 0.0, 1.0).astype(f32)
        x = wb[...]
        fc = dot(afac[...], x)
        wface = wf[now]
        send[t, 0] = fc[0:FP]
        send[t, 1] = fc[FP:2 * FP] + potf[...] * wface

        @pl.when(d < ND - 1)
        def _():
            up(t, d + 1).start()

        @pl.when(d > 0)
        def _():
            down(t, d - 1).start()

        ybuf[...] = dot(amat[...], x)

        @pl.when(d > 0)
        def _():
            up(t, d).wait_recv()
            down(t, d).wait_send()

        @pl.when(d < ND - 1)
        def _():
            down(t, d).wait_recv()
            up(t, d).wait_send()

        got = recv[t]
        wf[then] = coef * (send[t, 1] + got[0:FP] - 9.0 * wface) - keep * wf[then]
        hi, lo = split2(got)
        rb[:, 0:128] = hi
        rb[:, 128:256] = lo
        z = dot(bmat[...], rb[...])
        total = (ybuf[...] + z[:, 0:128] + z[:, 128:256]) * msk[...]
        new = coef * (total + (potc[...] - 9.0) * ws[now]) - keep * ws[then]
        ws[then] = new
        wb[...] = new.astype(bf16)
        return carry

    lax.fori_loop(0, DEGREE, step, 0)

    @pl.when(d > 0)
    def _():
        vcopy(d).wait_send()

    hi, lo = split2(ws[DEGREE % 2])
    back = dot(gt[...], jnp.concatenate([hi, lo], axis=1))
    hi, lo = split2(wf[DEGREE % 2])
    pad = jnp.zeros((256 - FP, 256), bf16)
    fback = dot(ft[...], jnp.concatenate([jnp.concatenate([hi, lo], axis=1), pad], axis=0))
    summed = (back + fback)[0:OWNED]
    count = cnt[0:OWNED, :]
    x = (potb[0:OWNED, :] - 9.0) * 0.125
    x2 = x * x
    alone = ((32.0 * x2 - 48.0) * x2 + 18.0) * x2 - 1.0
    out_ref[...] = jnp.where(count > 0.5, (summed[:, 0:128] + summed[:, 128:256]) / jnp.maximum(count, 1.0), alone * v_ref[...])


def filtered_states(states, potential, cell_matrix, connectivity, face_rows):
    V = pltpu.VMEM
    scratch = [
        V((8, CS), f32), V((8, 256), f32), V((CS, 128), i32), V((256, 128), i32), V((ROWS, 128), f32),
        V((CP, CP), bf16), V((CS, CS), bf16), V((2 * FP, CS), bf16), V((CS, 512), bf16), V((ROWS, CS), bf16),
        V((ROWS, 256), bf16), V((CS, ROWS), bf16), V((ROWS, 640), bf16), V((CS, 128), f32), V((FP, 128), f32),
        V((CS, 128), f32), V((ROWS, 128), f32), V((2, CS, COLS), f32), V((CS, COLS), bf16), V((2, FP, COLS), f32),
        V((CS, COLS), f32), V((512, 256), bf16), V((DEGREE, 2, FP, COLS), f32), V((DEGREE, 512, COLS), f32),
        V((FP, COLS), f32), V((256, COLS), f32),
        pltpu.SemaphoreType.DMA((DEGREE, 2)), pltpu.SemaphoreType.DMA((DEGREE, 2)), pltpu.SemaphoreType.DMA((2,)),
    ]
    return pl.pallas_call(
        filter_kernel,
        out_shape=jax.ShapeDtypeStruct((OWNED, COLS), f32),
        in_specs=[VM] * 5,
        out_specs=VM,
        scratch_shapes=scratch,
        compiler_params=pltpu.CompilerParams(collective_id=0, has_side_effects=True, vmem_limit_bytes=60 << 20),
        name="filter",
    )(states, potential.reshape(1, OWNED), cell_matrix, connectivity, face_rows)
HIGH = lax.Precision.HIGHEST


def nt(a, b, precision=None):
    return lax.dot_general(a, b, (((1,), (1,)), ((), ())), preferred_element_type=f32, precision=precision)


def nn(a, b):
    return jnp.dot(a, b, preferred_element_type=f32, precision=HIGH)


def chol_inverse(block):
    n = 128
    lane = lanes((8, n))
    sub = subs((8, n))
    a = [block[8 * k:8 * k + 8, :] for k in range(n // 8)]
    for j in range(n - 1):
        g, s = j // 8, j % 8
        row = a[g][s:s + 1, :]
        at_j = lane[0:1] == j
        scaled = jnp.where(at_j, 1.0, row) / row[:, j:j + 1]
        for k in range(g, n // 8):
            if k == g and s == 7:
                continue
            col = a[k][:, j:j + 1]
            upd = jnp.where(lane == j, 0.0, a[k]) - col * scaled
            a[k] = jnp.where(sub > s, upd, a[k]) if k == g else upd
    out = []
    for k in range(n // 8):
        here = sub + 8 * k
        diag = jnp.sum(jnp.where(lane == here, a[k], 0.0), axis=1, keepdims=True)
        unit = jnp.where(lane < here, a[k], jnp.where(lane == here, 1.0, 0.0))
        out.append(unit * lax.rsqrt(diag))
    return jnp.concatenate(out, axis=0)


def solve(ext, inv, zbuf, band):
    for i in range(4):
        a, b = 128 * i, 128 * i + 128
        t = chol_inverse(ext[a:b, a:b])
        inv[i] = t
        low = nt(ext[b:640, a:b], t, HIGH)
        ext[b:640, a:b] = low
        if i < 3:
            ext[b:640, b:512] = ext[b:640, b:512] - nt(low, low[0:512 - b], HIGH)
    eye = jnp.where(lanes((128, 128)) == subs((128, 128)), 1.0, 0.0)
    for i in (3, 2, 1, 0):
        a, b = 128 * i, 128 * i + 128
        y = jnp.where(band < 4, jnp.where(band == i, -eye, 0.0), ext[512:640, a:b])
        if i < 3:
            y = y - nn(zbuf[:, b:512], ext[b:512, a:b])
        zbuf[:, a:b] = nn(y, inv[i])


def peer(axis, index):
    return {axis: index}


def ortho(own_ref, mass_ref, out_ref, d, band, wgt, pan, wt, sbuf, rsbuf, agbuf, gbuf, ext, inv, zbuf, wcol,
          asem_s, asem_r, bsem_s, bsem_r, csem_s, csem_r, dsem_s, dsem_r, fsem_s,
          rs_s, rs_r, gg_s, gg_r, gm_s, gm_r, gx_s, gx_r, gy_s, gy_r):
    x = band // 4
    yh = lax.rem(band // 2, 2)
    c = lax.rem(band, 2)
    mine = lax.rem(band, 4)
    half = ROWS // 2

    def copy(src, dst, ss, rs, to):
        return pltpu.make_async_remote_copy(src_ref=src, dst_ref=dst, send_sem=ss, recv_sem=rs,
                                            device_id={"band": to}, device_id_type=MESHID)

    def part(block, h):
        return pan.at[block, pl.ds(h * half, half), :]

    def acopy(h, slot, to):
        return copy(part(mine, h), part(mine, h), asem_s.at[slot, h], asem_r.at[h], to)

    y_peer = x * 4 + (1 - yh) * 2 + c
    c_peer = x * 4 + yh * 2 + (1 - c)
    across = (1 - yh) * 2 + c
    own = own_ref[0:OWNED, :]

    @pl.when(x == 0)
    def _():
        pan[mine, 0:OWNED, :] = own.astype(bf16)
        pan[mine, OWNED:ROWS, :] = jnp.zeros((ROWS - OWNED, COLS), bf16)
        acopy(0, 0, band + 4).start()
        acopy(1, 1, band + 12).start()
        acopy(1, 0, band + 4).start()
        acopy(0, 1, band + 12).start()

    first = jnp.where(x == 3, 1, 0)

    def bcopy(h):
        return copy(part(mine, h), part(mine, h), bsem_s.at[h], bsem_r.at[h], y_peer)

    def ccopy(h):
        return copy(part(mine, h), part(mine, h), csem_s.at[h], csem_r.at[h], c_peer)

    def dcopy(h):
        return copy(part(across, h), part(across, h), dsem_s.at[h], dsem_r.at[h], c_peer)

    for k in range(2):
        h = lax.rem(first + k, 2)

        @pl.when(x > 0)
        def _():
            acopy(h, 0, band).wait_recv()

        if k == 0:
            @pl.when((x == 1) | (x == 3))
            def _():
                copy(part(mine, h), part(mine, h), fsem_s.at[0], asem_r.at[h], lax.rem(band, 4) + 8).start()
        bcopy(h).start()
        ccopy(h).start()

    for t in range(10):
        lo_row, hi_row = 128 * t, min(128 * t + 128, OWNED)
        if hi_row - lo_row == 128:
            row = mass_ref[0:1, lo_row:hi_row]
            wgt[lo_row:hi_row, :] = jnp.broadcast_to(row, (128, 128)).T * (1.0 / (ND * OWNED))
        else:
            wgt[lo_row:ROWS, :] = jnp.zeros((ROWS - lo_row, 128), f32)
            row = mass_ref[0:1, OWNED - 128:OWNED]
            wgt[OWNED - 128:OWNED, :] = jnp.broadcast_to(row, (128, 128)).T * (1.0 / (ND * OWNED))
    wcol[0:OWNED, :] = own * wgt[0:OWNED, :]
    wcol[OWNED:ROWS, :] = jnp.zeros((ROWS - OWNED, COLS), f32)
    for t in range(10):
        hi, lo = split2(wcol[128 * t:128 * t + 128, :].T)
        wt[0:128, 128 * t:128 * t + 128] = hi
        wt[128:256, 128 * t:128 * t + 128] = lo

    for k in range(2):
        h = lax.rem(first + k, 2)
        copy(part(across, h), part(across, h), bsem_s.at[h], bsem_r.at[h], y_peer).wait_recv()
        dcopy(h).start()
    for h in range(2):
        copy(part(mine, h), part(mine, h), csem_s.at[h], csem_r.at[h], c_peer).wait_recv()
        copy(part(mine, h), part(mine, h), dsem_s.at[h], dsem_r.at[h], c_peer).wait_recv()

    wcol[...] = pan[x].astype(f32) * wgt[...]
    pair = [jnp.concatenate([pan[0], pan[1]], axis=1), jnp.concatenate([pan[2], pan[3]], axis=1)]
    for t in range(10):
        ext[0:128, 0:128] = wcol[128 * t:128 * t + 128, :].T
        hi, lo = split2(ext[pl.ds(pl.multiple_of(lax.rem(band, 4) * 32, 32), 32), 0:128])
        wt[256:288, 128 * t:128 * t + 128] = hi
        wt[288:320, 128 * t:128 * t + 128] = lo
    for q in range(2):
        r = dot(wt[...], pair[q])
        sbuf[:, 256 * q:256 * q + 256] = r[0:128] + r[128:256]
        ext[0:32, 256 * q:256 * q + 256] = r[256:288] + r[288:320]
    for m in range(ND):
        sbuf[8 * m:8 * m + 8, 512:640] = ext[8 * (m // 4):8 * (m // 4) + 8, 128 * (m % 4):128 * (m % 4) + 128]

    def rows(m):
        return pl.ds(pl.multiple_of(m * 8, 8), 8)

    def rs(src_rows, slot, ss, to):
        return pltpu.make_async_remote_copy(
            src_ref=sbuf.at[rows(src_rows), :], dst_ref=rsbuf.at[slot], send_sem=rs_s.at[ss], recv_sem=rs_r.at[slot],
            device_id={"domain": to}, device_id_type=MESHID)

    for k in range(1, ND):
        to = lax.rem(d + k, ND)
        rs(to, d, k, to).start()
    rsbuf[d] = sbuf[rows(d), :]
    for k in range(1, ND):
        frm = lax.rem(d + k, ND)
        rs(frm, frm, k, frm).wait_recv()
    total = rsbuf[0]
    for m in range(1, ND):
        total = total + rsbuf[m]
    agbuf[rows(d), :] = total

    def ag(col, width, who, ss, rr, k, to):
        view = agbuf.at[rows(who), pl.ds(col, width)]
        return pltpu.make_async_remote_copy(
            src_ref=view, dst_ref=view, send_sem=ss.at[k], recv_sem=rr.at[who],
            device_id={"domain": to}, device_id_type=MESHID)

    for k in range(1, ND):
        to = lax.rem(d + k, ND)
        ag(512, 128, d, gg_s, gg_r, k, to).start()
    for k in range(1, ND):
        to = lax.rem(d + k, ND)
        ag(0, 512, d, gm_s, gm_r, k, to).start()
    for k in range(1, ND):
        frm = lax.rem(d + k, ND)
        ag(512, 128, frm, gg_s, gg_r, k, frm).wait_recv()

    gbuf[band] = agbuf[:, 512:640]
    chip = band // 2

    def strip(who, ss, rr, k, to):
        return copy(gbuf.at[who], gbuf.at[who], ss.at[k], rr.at[who], to)

    for k in range(1, 8):
        to = lax.rem(chip + k, 8) * 2 + c
        strip(band, gx_s, gx_r, k, to).start()
    strip(band, gy_s, gy_r, 0, c_peer).start()
    for k in range(1, 8):
        frm = lax.rem(chip + k, 8) * 2 + c
        strip(frm, gx_s, gx_r, k, frm).wait_recv()
        strip(frm, gy_s, gy_r, k, c_peer).start()
    for k in range(8):
        frm = lax.rem(chip + k, 8) * 2 + (1 - c)
        strip(frm, gy_s, gy_r, k, c_peer).wait_recv()

    for b in range(16):
        for m in range(ND):
            ext[32 * b + 8 * (m // 4):32 * b + 8 * (m // 4) + 8, 128 * (m % 4):128 * (m % 4) + 128] = gbuf[b, 8 * m:8 * m + 8, :]
    for k in range(1, ND):
        frm = lax.rem(d + k, ND)
        ag(0, 512, frm, gm_s, gm_r, k, frm).wait_recv()
    ext[512:640, :] = agbuf[:, 0:512]

    solve(ext, inv, zbuf, band)

    zh, zl = split2(zbuf[...])
    zz = jnp.concatenate([zh, zl], axis=0)
    prod = nt(pair[0], zz[:, 0:256]) + nt(pair[1], zz[:, 256:512])
    update = prod[0:OWNED, 0:128] + prod[0:OWNED, 128:256]
    is_panel = band < 4
    zown = zbuf[:, pl.ds(pl.multiple_of(jnp.minimum(band, 3) * 128, 128), 128)]
    rest = (own - own.astype(bf16).astype(f32)).astype(bf16)
    fix = nt(rest, zown.astype(bf16))
    out_ref[...] = jnp.where(is_panel, -update - fix, own - update)

    @pl.when(x == 0)
    def _():
        for h in range(2):
            acopy(h, 0, band).wait_send()
            acopy(h, 1, band).wait_send()

    @pl.when((x == 1) | (x == 3))
    def _():
        copy(part(mine, 0), part(mine, 0), fsem_s.at[0], asem_r.at[0], band).wait_send()

    for h in range(2):
        bcopy(h).wait_send()
        ccopy(h).wait_send()
        dcopy(h).wait_send()
    for k in range(1, ND):
        rs(d, d, k, d).wait_send()
        ag(512, 128, d, gg_s, gg_r, k, d).wait_send()
        ag(0, 512, d, gm_s, gm_r, k, d).wait_send()
    for k in range(1, 8):
        strip(band, gx_s, gx_r, k, band).wait_send()
    for k in range(8):
        strip(band, gy_s, gy_r, k, band).wait_send()


def ortho_kernel(own_ref, mass_ref, out_ref, *scratch):
    d = lax.axis_index("domain")
    band = lax.axis_index("band")
    barrier = pltpu.get_barrier_semaphore()
    for k in range(1, 16):
        pl.semaphore_signal(barrier, inc=1, device_id={"domain": lax.rem(d + k, ND)}, device_id_type=MESHID)
        pl.semaphore_signal(barrier, inc=1, device_id={"band": lax.rem(band + k, 16)}, device_id_type=MESHID)
    pl.semaphore_wait(barrier, 30)
    ortho(own_ref, mass_ref, out_ref, d, band, *scratch)


def orthonormal_states(own, mass):
    V = pltpu.VMEM
    D = pltpu.SemaphoreType.DMA
    scratch = [
        V((ROWS, 128), f32), V((4, ROWS, COLS), bf16), V((320, ROWS), bf16), V((128, 640), f32), V((ND, 8, 640), f32),
        V((128, 640), f32), V((16, 128, 128), f32), V((640, 512), f32), V((4, 128, 128), f32), V((128, 512), f32),
        V((ROWS, COLS), f32),
        D((2, 2)), D((2,)), D((2,)), D((2,)), D((2,)), D((2,)), D((2,)), D((2,)), D((1,)),
        D((ND,)), D((ND,)), D((ND,)), D((ND,)), D((ND,)), D((ND,)), D((8,)), D((16,)), D((8,)), D((16,)),
    ]
    return pl.pallas_call(
        ortho_kernel,
        out_shape=jax.ShapeDtypeStruct((OWNED, COLS), f32),
        in_specs=[VM] * 2,
        out_specs=VM,
        scratch_shapes=scratch,
        compiler_params=pltpu.CompilerParams(collective_id=1, has_side_effects=True, vmem_limit_bytes=60 << 20),
        name="orthonormalize",
    )(own, mass.reshape(1, OWNED))


def per_device(states, potential, node_mass, cell_matrix, connectivity, face_rows):
    filtered = filtered_states(states, potential, cell_matrix, connectivity, face_rows)
    return orthonormal_states(filtered, node_mass)


def solution(mesh):
    return jax.shard_map(
        per_device, mesh=mesh,
        in_specs=(P("domain", "band"), P("domain"), P("domain"), P(), P("domain", None), P("domain", None)),
        out_specs=P("domain", "band"), check_vma=False,
    )
```

```python
import functools
import jax
import jax.numpy as jnp
from jax import lax
from jax.experimental import pallas as pl
from jax.experimental.pallas import tpu as pltpu
from jax.sharding import PartitionSpec as P

f32 = jnp.float32
bf16 = jnp.bfloat16
i32 = jnp.int32
OWNED = 1224
ROWS = 1280
CELL = 729
CP = 768
CS = 1536
FACE = 153
FP = 160
COLS = 128
DEGREE = 6
ND = 16
MESHID = pl.DeviceIdType.MESH
VM = pl.BlockSpec(memory_space=pltpu.VMEM)


def dot(a, b):
    return jnp.dot(a, b, preferred_element_type=f32)


def split2(x):
    hi = x.astype(bf16)
    return hi, (x - hi.astype(f32)).astype(bf16)


def split3(x):
    hi = x.astype(bf16)
    rest = x - hi.astype(f32)
    mid = rest.astype(bf16)
    return hi, mid, (rest - mid.astype(f32)).astype(bf16)


def lanes(shape, base=0):
    return lax.broadcasted_iota(i32, shape, 1) + base


def subs(shape, base=0):
    return lax.broadcasted_iota(i32, shape, 0) + base


def onehot(mask):
    return jnp.where(mask, 1.0, 0.0).astype(bf16)


HIGH = lax.Precision.HIGHEST


def nt(a, b, precision=None):
    return lax.dot_general(a, b, (((1,), (1,)), ((), ())), preferred_element_type=f32, precision=precision)


def nn(a, b):
    return jnp.dot(a, b, preferred_element_type=f32, precision=HIGH)


def chol_inverse(block):
    n = 128
    shape = (8, n)
    lane = lanes(shape)
    sub = subs(shape)
    a = [block[8 * k:8 * k + 8, :] for k in range(n // 8)]
    out = []
    for g in range(n // 8):
        j0 = 8 * g
        inside = (lane >= j0) & (lane < j0 + 8)
        here = a[g]
        cols = [jnp.broadcast_to(here[:, j0 + k:j0 + k + 1], shape) for k in range(8)]
        s = {(i, k): jnp.broadcast_to(cols[k][i:i + 1, :], shape) for k in range(8) for i in range(k, 8)}
        r = [jnp.where(inside, 0.0, jnp.broadcast_to(here[i:i + 1, :], shape)) for i in range(8)]
        inv, done = [], None
        for k in range(8):
            root = lax.rsqrt(s[k, k])
            inv.append(root * root)
            r[k] = jnp.where(lane == j0 + k, 1.0, r[k])
            for i in range(k + 1, 8):
                m = s[i, k] * inv[k]
                for q in range(k + 1, i + 1):
                    s[i, q] = s[i, q] - m * s[q, k]
                r[i] = r[i] - m * r[k]
            row = r[k] * root
            done = row if done is None else jnp.where(sub == k, row, done)
        out.append(jnp.where(lane <= sub + j0, done, 0.0))
        for t in range(g + 1, n // 8):
            c = [jnp.broadcast_to(a[t][:, j0 + k:j0 + k + 1], shape) for k in range(8)]
            acc = jnp.where(inside, 0.0, a[t])
            for k in range(8):
                m = c[k] * inv[k]
                for q in range(k + 1, 8):
                    c[q] = c[q] - m * s[q, k]
                acc = acc - m * r[k]
            a[t] = acc
    return jnp.concatenate(out, axis=0)


def factor(ext, inv):
    for i in range(4):
        a, b = 128 * i, 128 * i + 128
        t = chol_inverse(ext[a:b, a:b])
        inv[i] = t
        if i < 3:
            low = nt(ext[b:512, a:b], t, HIGH)
            ext[b:512, a:b] = low
            ext[b:512, b:512] = ext[b:512, b:512] - nt(low, low, HIGH)


def solve(ext, inv, m_ref, ybuf, zbuf, band):
    for i in range(4):
        a, b = 128 * i, 128 * i + 128
        y = m_ref[:, a:b]
        if i > 0:
            y = y - nt(ybuf[:, 0:a], ext[a:b, 0:a], HIGH)
        ybuf[:, a:b] = nt(y, inv[i], HIGH)
    eye = jnp.where(lanes((128, 128)) == subs((128, 128)), 1.0, 0.0)
    for i in (3, 2, 1, 0):
        a, b = 128 * i, 128 * i + 128
        y = jnp.where(band < 4, jnp.where(band == i, -eye, 0.0), ybuf[:, a:b])
        if i < 3:
            y = y - nn(zbuf[:, b:512], ext[b:512, a:b])
        zbuf[:, a:b] = nn(y, inv[i])


NCH = 6
CH = 208


def filter_states(d, barrier_wait, v_ref, pot_ref, mass_ref, mat_ref, conn_ref, face_ref, own,
                  crow, frow, connb, faceb, potb, kp, amat, afac, bmat, gt, ft, gsel, v3, potc, potf, msk,
                  cnt, ws, wb, wf, ybuf, send, recv, vsend, vrecv, ssem, rsem, vsem, wgt):
    crow[...] = jnp.full(crow.shape, -1.0, f32)
    crow[0:1, 0:CELL] = conn_ref[0:1, :].astype(f32)
    crow[0:1, CP:CP + CELL] = conn_ref[1:2, :].astype(f32)
    frow[...] = jnp.full(frow.shape, -2.0, f32)
    frow[0:1, 0:FACE] = face_ref[0:1, :].astype(f32)
    for t in range(2):
        row = frow[0:1, 128 * t:128 * t + 128]
        faceb[128 * t:128 * t + 128, :] = jnp.broadcast_to(row, (128, 128)).T.astype(i32)
    potb[1152:1280, :] = jnp.zeros((128, 128), f32)
    v3[1216:ROWS, :] = jnp.zeros((ROWS - 1216, 512), bf16)
    for t in range(9):
        row = pot_ref[0:1, 128 * t:128 * t + 128]
        potb[128 * t:128 * t + 128, :] = jnp.broadcast_to(row, (128, 128)).T
    potb[OWNED - 128:OWNED, :] = jnp.broadcast_to(pot_ref[0:1, OWNED - 128:OWNED], (128, 128)).T
    hi, lo = split2(v_ref[...])
    v3[0:OWNED, 0:128] = hi
    v3[0:OWNED, 128:256] = lo
    hi, lo = split2(potb[0:OWNED, :])
    v3[0:OWNED, 256:384] = hi
    v3[0:OWNED, 384:512] = lo

    fsel = onehot(jnp.tile(faceb[0:FP, :], (1, ROWS // 128)) == lanes((FP, ROWS)))
    fv = dot(fsel, v3[...])
    vface = fv[:, 0:128] + fv[:, 128:256]
    potf[...] = fv[:, 256:384] + fv[:, 384:512]
    wf[0] = vface
    wf[1] = jnp.zeros((FP, COLS), f32)
    vsend[...] = vface.astype(bf16)
    ws[1] = jnp.zeros((CS, COLS), f32)
    barrier_wait()

    def vcopy(dst):
        return pltpu.make_async_remote_copy(
            src_ref=vsend, dst_ref=vrecv.at[pl.ds(0, FP), :], send_sem=vsem.at[0], recv_sem=vsem.at[1],
            device_id={"domain": dst}, device_id_type=MESHID)

    @pl.when(d > 0)
    def _():
        vcopy(d - 1).start()

    for t in range(CS // 128):
        row = crow[0:1, 128 * t:128 * t + 128]
        connb[128 * t:128 * t + 128, :] = jnp.broadcast_to(row, (128, 128)).T.astype(i32)
    kp[...] = jnp.zeros(kp.shape, bf16)
    kp[0:CELL, 0:CELL] = mat_ref[...]
    ci = crow[0:1, :].astype(i32)
    fi = frow[0:1, :].astype(i32)
    tup = onehot(subs((FP, CS), OWNED) == ci)
    tlo = onehot(jnp.tile(faceb[0:FP, :], (1, CS // 128)) == ci)
    both = jnp.concatenate([tup, tlo], axis=0)
    for c in range(2):
        cols = slice(CP * c, CP * c + CP)
        afac[:, cols] = dot(both[:, cols], kp[...]).astype(bf16)
    for t in range(ROWS // 128):
        gsel[:, 128 * t:128 * t + 128] = onehot(connb[...] == lanes((CS, 128), 128 * t))
    cv = dot(gsel[...], v3[...])
    ws[0] = cv[:, 0:128] + cv[:, 128:256]
    potc[...] = cv[:, 256:384] + cv[:, 384:512]
    cb2 = jnp.tile(connb[...], (1, 2))
    bmat[:, 0:256] = onehot(cb2 == fi)
    bmat[:, 256:512] = onehot(cb2 == lanes((CS, 256), OWNED))
    msk[...] = jnp.where((connb[...] >= OWNED) & (d == ND - 1), 0.0, 1.0)

    @pl.when(d < ND - 1)
    def _():
        vcopy(d).wait_recv()

    first = ws[0] + dot(bmat[:, 256:512], vrecv[...])
    ws[0] = first
    wb[...] = first.astype(bf16)

    def up(t, dst):
        return pltpu.make_async_remote_copy(
            src_ref=send.at[t, 0], dst_ref=recv.at[t, pl.ds(0, FP), :], send_sem=ssem.at[t, 0], recv_sem=rsem.at[t, 0],
            device_id={"domain": dst}, device_id_type=MESHID)

    def down(t, dst):
        return pltpu.make_async_remote_copy(
            src_ref=send.at[t, 1], dst_ref=recv.at[t, pl.ds(256, FP), :], send_sem=ssem.at[t, 1], recv_sem=rsem.at[t, 1],
            device_id={"domain": dst}, device_id_type=MESHID)

    def step(t, carry):
        now, then = lax.rem(t, 2), lax.rem(t + 1, 2)
        coef = jnp.where(t == 0, 0.125, 0.25).astype(f32)
        keep = jnp.where(t == 0, 0.0, 1.0).astype(f32)
        x = wb[...]
        fc = dot(afac[...], x)
        wface = wf[now]
        lower = fc[FP:2 * FP] + potf[...] * wface
        send[t, 0] = fc[0:FP].astype(bf16)
        send[t, 1] = lower.astype(bf16)

        @pl.when(d < ND - 1)
        def _():
            up(t, d + 1).start()

        @pl.when(d > 0)
        def _():
            down(t, d - 1).start()

        @pl.when(t == 0)
        def _():
            km = kp[...]
            amat[0:CP, 0:CP] = km
            amat[CP:CS, CP:CS] = km
            none = jnp.zeros((CP, CP), bf16)
            c0 = jnp.tile(connb[0:CP, :], (1, CP // 128))
            e01 = jnp.where(c0 >= 0, onehot(c0 == crow[0:1, CP:CS].astype(i32)), none)
            amat[0:CP, CP:CS] = dot(e01, km).astype(bf16)
            c1 = jnp.tile(connb[CP:CS, :], (1, CP // 128))
            e10 = jnp.where(c1 >= 0, onehot(c1 == crow[0:1, 0:CP].astype(i32)), none)
            amat[CP:CS, 0:CP] = dot(e10, km).astype(bf16)

        ybuf[...] = dot(amat[...], x)

        @pl.when(t < 5)
        def _():
            at = pl.ds(pl.multiple_of(256 * t, 256), 256)
            g = onehot(subs((256, CS), 256 * t) == ci)
            h = onehot(subs((256, 256), 256 * t) == fi)
            gt[at, :] = g
            ft[at, :] = h
            cnt[at, :] = dot(g, jnp.ones((CS, COLS), bf16)) + dot(h, jnp.ones((256, COLS), bf16))

        @pl.when(t == 5)
        def _():
            for s in range(9):
                row = mass_ref[0:1, 128 * s:128 * s + 128]
                wgt[128 * s:128 * s + 128, :] = jnp.broadcast_to(row, (128, 128)).T * (1.0 / (ND * OWNED))
            wgt[1152:ROWS, :] = jnp.zeros((ROWS - 1152, 128), f32)
            row = mass_ref[0:1, OWNED - 128:OWNED]
            wgt[OWNED - 128:OWNED, :] = jnp.broadcast_to(row, (128, 128)).T * (1.0 / (ND * OWNED))

        @pl.when(d > 0)
        def _():
            up(t, d).wait_recv()
            down(t, d).wait_send()

        @pl.when(d < ND - 1)
        def _():
            down(t, d).wait_recv()
            up(t, d).wait_send()

        got = recv[t]
        wf[then] = coef * (lower + got[0:FP].astype(f32) - 9.0 * wface) - keep * wf[then]
        total = (ybuf[...] + dot(bmat[...], got)) * msk[...]
        new = coef * (total + (potc[...] - 9.0) * ws[now]) - keep * ws[then]
        ws[then] = new
        wb[...] = new.astype(bf16)
        return carry

    lax.fori_loop(0, DEGREE, step, 0)

    @pl.when(d > 0)
    def _():
        vcopy(d).wait_send()

    hi, lo = split2(ws[DEGREE % 2])
    back = dot(gt[...], jnp.concatenate([hi, lo], axis=1))
    hi, lo = split2(wf[DEGREE % 2])
    pad = jnp.zeros((256 - FP, 256), bf16)
    fback = dot(ft[...], jnp.concatenate([jnp.concatenate([hi, lo], axis=1), pad], axis=0))
    summed = (back + fback)[0:OWNED]
    count = cnt[0:OWNED, :]
    x = (potb[0:OWNED, :] - 9.0) * 0.125
    x2 = x * x
    alone = ((32.0 * x2 - 48.0) * x2 + 18.0) * x2 - 1.0
    own[0:OWNED, :] = jnp.where(count > 0.5, (summed[:, 0:128] + summed[:, 128:256]) / jnp.maximum(count, 1.0), alone * v_ref[...])
    own[OWNED:ROWS, :] = jnp.zeros((ROWS - OWNED, COLS), f32)


def strip_of(band):
    x = band // 4
    return 4 * (2 * lax.rem(band // 2, 2) + x // 2) + lax.rem(x, 2) * 2 + lax.rem(band, 2)


def ortho(own_ref, out_ref, d, band, wgt, pan, wt, sbm, rsm, sbg, rsg, agg, agm, gbuf, stripbuf, ext, inv, ybuf, zbuf, wcol,
          asem_s, asem_r, bsem_s, bsem_r, csem_s, csem_r, dsem_s, dsem_r, fsem_s,
          rg_s, rg_r, rm_s, rm_r, gg_s, gg_r, gm_s, gm_r, gx_s, gx_r, gy_s, gy_r):
    x = band // 4
    yh = lax.rem(band // 2, 2)
    c = lax.rem(band, 2)
    mine = lax.rem(band, 4)

    def copy(src, dst, ss, rs, to):
        return pltpu.make_async_remote_copy(src_ref=src, dst_ref=dst, send_sem=ss, recv_sem=rs,
                                            device_id={"band": to}, device_id_type=MESHID)

    def part(block, h):
        return pan.at[block, pl.ds(pl.multiple_of(h * CH, 16), CH), :]

    def acopy(h, slot, to):
        return copy(part(mine, h), part(mine, h), asem_s.at[slot, h], asem_r.at[h], to)

    y_peer = x * 4 + (1 - yh) * 2 + c
    c_peer = x * 4 + yh * 2 + (1 - c)
    across = (1 - yh) * 2 + c

    @pl.when(x == 0)
    def _():
        pan[mine, 0:NCH * CH, :] = own_ref[0:NCH * CH, :].astype(bf16)
        for k in range(NCH):
            acopy(k, 0, band + 4).start()
            acopy((k + 3) % NCH, 1, band + 12).start()

    def order(k):
        return jnp.where(x == 3, (k + 3) % NCH, jnp.where(x == 2, (k % 2) * 3 + k // 2, k))

    def bcopy(h):
        return copy(part(mine, h), part(mine, h), bsem_s.at[h], bsem_r.at[h], y_peer)

    def ccopy(h):
        return copy(part(mine, h), part(mine, h), csem_s.at[h], csem_r.at[h], c_peer)

    def dcopy(h):
        return copy(part(across, h), part(across, h), dsem_s.at[h], dsem_r.at[h], c_peer)

    def fcopy(h, k, to):
        return copy(part(mine, h), part(mine, h), fsem_s.at[k], asem_r.at[h], to)

    for k in range(NCH):
        h = order(k)

        @pl.when(x > 0)
        def _():
            acopy(h, 0, band).wait_recv()

        if k < 3:
            @pl.when((x == 1) | (x == 3))
            def _():
                fcopy(h, k, mine + 8).start()
        bcopy(h).start()
        ccopy(h).start()

    for t in range(10):
        at = slice(128 * t, 128 * t + 128)
        hi, lo = split2((own_ref[at, :] * wgt[at, :]).T)
        wt[0:128, at] = hi
        wt[128:256, at] = lo

    for h in range(NCH):
        copy(part(mine, h), part(mine, h), csem_s.at[h], csem_r.at[h], c_peer).wait_recv()
    wcol[...] = pan[2 * yh + x // 2].astype(f32) * wgt[...]
    sub = pl.multiple_of((lax.rem(x, 2) * 2 + c) * 32, 32)
    for t in range(10):
        at = slice(128 * t, 128 * t + 128)
        ybuf[0:128, 0:128] = wcol[at, :].T
        hi, lo = split2(ybuf[pl.ds(sub, 32), 0:128])
        wt[256:288, at] = hi
        wt[288:320, at] = lo

    def rows(m):
        return pl.ds(pl.multiple_of(m * 8, 8), 8)

    def rm(p, src_rows, slot, ss, to):
        return pltpu.make_async_remote_copy(
            src_ref=sbm.at[p, rows(src_rows), :], dst_ref=rsm.at[p, slot], send_sem=rm_s.at[p, ss], recv_sem=rm_r.at[p, slot],
            device_id={"domain": to}, device_id_type=MESHID)

    def rg(src_rows, slot, ss, to):
        return pltpu.make_async_remote_copy(
            src_ref=sbg.at[rows(src_rows), :], dst_ref=rsg.at[slot], send_sem=rg_s.at[ss], recv_sem=rg_r.at[slot],
            device_id={"domain": to}, device_id_type=MESHID)

    def products(p, panel):
        both = jnp.concatenate([pan[2 * panel], pan[2 * panel + 1]], axis=1)
        r = dot(wt[...], both)
        sbm[p] = r[0:128] + r[128:256]
        stripbuf[:, pl.ds(pl.multiple_of(panel * 256, 256), 256)] = r[256:288] + r[288:320]

    products(0, yh)
    for k in range(1, ND):
        to = lax.rem(d + k, ND)
        rm(0, to, d, k, to).start()

    for k in range(NCH):
        h = order(k)
        copy(part(across, h), part(across, h), bsem_s.at[h], bsem_r.at[h], y_peer).wait_recv()
        dcopy(h).start()
    for h in range(NCH):
        copy(part(mine, h), part(mine, h), dsem_s.at[h], dsem_r.at[h], c_peer).wait_recv()

    products(1, 1 - yh)
    for m in range(ND):
        sbg[8 * m:8 * m + 8, :] = stripbuf[8 * (m // 4):8 * (m // 4) + 8, 128 * (m % 4):128 * (m % 4) + 128]
    for k in range(1, ND):
        to = lax.rem(d + k, ND)
        rg(to, d, k, to).start()
    for k in range(1, ND):
        to = lax.rem(d + k, ND)
        rm(1, to, d, k, to).start()
    rsg[d] = sbg[rows(d), :]
    rsm[0, d] = sbm[0, rows(d), :]
    rsm[1, d] = sbm[1, rows(d), :]
    for k in range(1, ND):
        frm = lax.rem(d + k, ND)
        rg(frm, frm, k, frm).wait_recv()
    total = rsg[0]
    for m in range(1, ND):
        total = total + rsg[m]
    agg[rows(d), :] = total

    def ag(buf, who, ss, rr, k, to):
        view = buf.at[rows(who), :]
        return pltpu.make_async_remote_copy(
            src_ref=view, dst_ref=view, send_sem=ss.at[k], recv_sem=rr.at[who],
            device_id={"domain": to}, device_id_type=MESHID)

    for k in range(1, ND):
        to = lax.rem(d + k, ND)
        ag(agg, d, gg_s, gg_r, k, to).start()
    for p in range(2):
        for k in range(1, ND):
            frm = lax.rem(d + k, ND)
            rm(p, frm, frm, k, frm).wait_recv()
        total = rsm[p, 0]
        for m in range(1, ND):
            total = total + rsm[p, m]
        panel = yh if p == 0 else 1 - yh
        agm[rows(d), pl.ds(pl.multiple_of(panel * 256, 256), 256)] = total
    for k in range(1, ND):
        frm = lax.rem(d + k, ND)
        ag(agg, frm, gg_s, gg_r, k, frm).wait_recv()

    here = strip_of(band)
    gbuf[here] = agg[...]
    chip = band // 2

    def strip(who, ss, rr, k, to):
        return copy(gbuf.at[who], gbuf.at[who], ss.at[k], rr.at[who], to)

    for k in range(1, 8):
        to = lax.rem(chip + k, 8) * 2 + c
        strip(here, gx_s, gx_r, k, to).start()
    strip(here, gy_s, gy_r, 0, c_peer).start()
    for k in range(1, ND):
        to = lax.rem(d + k, ND)
        ag(agm, d, gm_s, gm_r, k, to).start()
    for k in range(1, 8):
        frm = strip_of(lax.rem(chip + k, 8) * 2 + c)
        strip(frm, gx_s, gx_r, k, c_peer).wait_recv()
        strip(frm, gy_s, gy_r, k, c_peer).start()
    for k in range(8):
        frm = strip_of(lax.rem(chip + k, 8) * 2 + (1 - c))
        strip(frm, gy_s, gy_r, k, c_peer).wait_recv()

    for b in range(16):
        for m in range(ND):
            ext[32 * b + 8 * (m // 4):32 * b + 8 * (m // 4) + 8, 128 * (m % 4):128 * (m % 4) + 128] = gbuf[b, 8 * m:8 * m + 8, :]

    factor(ext, inv)
    for k in range(1, ND):
        frm = lax.rem(d + k, ND)
        ag(agm, frm, gm_s, gm_r, k, frm).wait_recv()
    solve(ext, inv, agm, ybuf, zbuf, band)

    own = own_ref[0:OWNED, :]
    zh, zl = split2(zbuf[...])
    zz = jnp.concatenate([zh, zl], axis=0)
    pair = [jnp.concatenate([pan[0], pan[1]], axis=1), jnp.concatenate([pan[2], pan[3]], axis=1)]
    prod = nt(pair[0], zz[:, 0:256]) + nt(pair[1], zz[:, 256:512])
    update = prod[0:OWNED, 0:128] + prod[0:OWNED, 128:256]
    is_panel = band < 4
    zown = zbuf[:, pl.ds(pl.multiple_of(jnp.minimum(band, 3) * 128, 128), 128)]
    rest = (own - own.astype(bf16).astype(f32)).astype(bf16)
    fix = nt(rest, zown.astype(bf16))
    out_ref[...] = jnp.where(is_panel, -update - fix, own - update)

    @pl.when(x == 0)
    def _():
        for h in range(NCH):
            acopy(h, 0, y_peer).wait_send()
            acopy(h, 1, y_peer).wait_send()

    @pl.when((x == 1) | (x == 3))
    def _():
        for k in range(3):
            fcopy(0, k, y_peer).wait_send()

    for h in range(NCH):
        bcopy(h).wait_send()
        ccopy(h).wait_send()
        dcopy(h).wait_send()
    for k in range(1, ND):
        to = lax.rem(d + k, ND)
        rg(d, d, k, to).wait_send()
        rm(0, d, d, k, to).wait_send()
        rm(1, d, d, k, to).wait_send()
        ag(agg, d, gg_s, gg_r, k, to).wait_send()
        ag(agm, d, gm_s, gm_r, k, to).wait_send()
    for k in range(1, 8):
        strip(here, gx_s, gx_r, k, c_peer).wait_send()
    for k in range(8):
        strip(here, gy_s, gy_r, k, c_peer).wait_send()


def kernel(v_ref, pot_ref, mass_ref, mat_ref, conn_ref, face_ref, out_ref, own, wgt, vrecv, recv, pan, *scratch):
    d = lax.axis_index("domain")
    band = lax.axis_index("band")
    vrecv[...] = jnp.zeros(vrecv.shape, bf16)
    recv[...] = jnp.zeros(recv.shape, bf16)
    for j in range(4):
        pan[j, NCH * CH:ROWS, :] = jnp.zeros((ROWS - NCH * CH, COLS), bf16)
    barrier = pltpu.get_barrier_semaphore()
    for k in range(1, 16):
        pl.semaphore_signal(barrier, inc=1, device_id={"domain": lax.rem(d + k, ND)}, device_id_type=MESHID)
        pl.semaphore_signal(barrier, inc=1, device_id={"band": lax.rem(band + k, 16)}, device_id_type=MESHID)
    n = len(FILTER)
    f = scratch[:n]
    filter_states(d, lambda: pl.semaphore_wait(barrier, 30), v_ref, pot_ref, mass_ref, mat_ref, conn_ref, face_ref, own,
                  *f[:22], recv, f[22], vrecv, *f[23:], wgt)
    ortho(own, out_ref, d, band, wgt, pan, *scratch[n:])


V = pltpu.VMEM
D = pltpu.SemaphoreType.DMA
FILTER = (
    V((8, CS), f32), V((8, 256), f32), V((CS, 128), i32), V((256, 128), i32), V((ROWS, 128), f32),
    V((CP, CP), bf16), V((CS, CS), bf16), V((2 * FP, CS), bf16), V((CS, 512), bf16), V((ROWS, CS), bf16),
    V((ROWS, 256), bf16), V((CS, ROWS), bf16), V((ROWS, 512), bf16), V((CS, 128), f32), V((FP, 128), f32),
    V((CS, 128), f32), V((ROWS, 128), f32), V((2, CS, COLS), f32), V((CS, COLS), bf16), V((2, FP, COLS), f32),
    V((CS, COLS), f32),
    V((DEGREE, 2, FP, COLS), bf16), V((FP, COLS), bf16),
    D((DEGREE, 2)), D((DEGREE, 2)), D((2,)),
)
ORTHO = (
    V((320, ROWS), bf16), V((2, 128, 256), f32), V((2, ND, 8, 256), f32), V((128, 128), f32), V((ND, 8, 128), f32),
    V((128, 128), f32), V((128, 512), f32), V((16, 128, 128), f32), V((32, 512), f32), V((512, 512), f32), V((4, 128, 128), f32),
    V((128, 512), f32), V((128, 512), f32), V((ROWS, COLS), f32),
    D((2, NCH)), D((NCH,)), D((NCH,)), D((NCH,)), D((NCH,)), D((NCH,)), D((NCH,)), D((NCH,)), D((3,)),
    D((ND,)), D((ND,)), D((2, ND)), D((2, ND)), D((ND,)), D((ND,)), D((ND,)), D((ND,)), D((8,)), D((16,)), D((8,)), D((16,)),
)
SHARED = (V((ROWS, COLS), f32), V((ROWS, 128), f32), V((256, COLS), bf16), V((DEGREE, 512, COLS), bf16), V((4, ROWS, COLS), bf16))


def per_device(states, potential, node_mass, cell_matrix, connectivity, face_rows):
    return pl.pallas_call(
        kernel,
        out_shape=jax.ShapeDtypeStruct((OWNED, COLS), f32),
        in_specs=[VM] * 6,
        out_specs=VM,
        scratch_shapes=list(SHARED + FILTER + ORTHO),
        compiler_params=pltpu.CompilerParams(collective_id=0, has_side_effects=True, vmem_limit_bytes=60 << 20),
        name="subspace",
    )(states, potential.reshape(1, OWNED), node_mass.reshape(1, OWNED), cell_matrix, connectivity, face_rows)


def solution(mesh):
    return jax.shard_map(
        per_device, mesh=mesh,
        in_specs=(P("domain", "band"), P("domain"), P("domain"), P(), P("domain", None), P("domain", None)),
        out_specs=P("domain", "band"), check_vma=False,
    )
```

```python
import functools
import jax
import jax.numpy as jnp
from jax import lax
from jax.experimental import pallas as pl
from jax.experimental.pallas import tpu as pltpu
from jax.sharding import PartitionSpec as P

f32 = jnp.float32
bf16 = jnp.bfloat16
i32 = jnp.int32
OWNED = 1224
ROWS = 1280
CELL = 729
CP = 768
CS = 1536
FACE = 153
FP = 160
COLS = 128
DEGREE = 6
ND = 16
MESHID = pl.DeviceIdType.MESH
VM = pl.BlockSpec(memory_space=pltpu.VMEM)


def dot(a, b):
    return jnp.dot(a, b, preferred_element_type=f32)


def split2(x):
    hi = x.astype(bf16)
    return hi, (x - hi.astype(f32)).astype(bf16)


def split3(x):
    hi = x.astype(bf16)
    rest = x - hi.astype(f32)
    mid = rest.astype(bf16)
    return hi, mid, (rest - mid.astype(f32)).astype(bf16)


def lanes(shape, base=0):
    return lax.broadcasted_iota(i32, shape, 1) + base


def subs(shape, base=0):
    return lax.broadcasted_iota(i32, shape, 0) + base


def onehot(mask):
    return jnp.where(mask, 1.0, 0.0).astype(bf16)


HIGH = lax.Precision.HIGHEST


def nt(a, b, precision=None):
    return lax.dot_general(a, b, (((1,), (1,)), ((), ())), preferred_element_type=f32, precision=precision)


def nn(a, b):
    return jnp.dot(a, b, preferred_element_type=f32, precision=HIGH)


def chol_inverse(block):
    n, groups = 128, 16
    shape = (8, n)
    lane = lanes(shape)
    sub = subs(shape)

    def spread(x, j):
        return jnp.broadcast_to(x[:, j:j + 1], shape)

    def pick(x, i):
        return jnp.take_along_axis(x, jnp.full(shape, i, i32), axis=0)

    a = [block[8 * k:8 * k + 8, :] for k in range(groups)]
    out = []
    diag = [spread(a[0], q) for q in range(8)]
    below = [spread(a[1], q) for q in range(8)]
    ahead = [spread(a[1], 8 + q) for q in range(8)]
    for g in range(groups):
        j0 = 8 * g
        inside = (lane >= j0) & (lane < j0 + 8)
        s = {(i, k): pick(diag[k], i) for k in range(8) for i in range(k, 8)}
        r = [jnp.where(inside, 0.0, pick(a[g], i)) for i in range(8)]
        near = range(g + 2, min(g + 4, groups))
        side = {t: [spread(a[t], j0 + k) for k in range(8)] for t in near}
        inv, done, mult = [], None, None
        acc = jnp.where(inside, 0.0, a[g + 1]) if g + 1 < groups else None
        for k in range(8):
            root = lax.rsqrt(s[k, k])
            inv.append(root * root)
            r[k] = jnp.where(lane == j0 + k, 1.0, r[k])
            for i in range(k + 1, 8):
                m = s[i, k] * inv[k]
                for q in range(k + 1, i + 1):
                    s[i, q] = s[i, q] - m * s[q, k]
                r[i] = r[i] - m * r[k]
            if g + 1 < groups:
                m = below[k] * inv[k]
                for q in range(8):
                    ahead[q] = ahead[q] - m * pick(below[k], q)
                for q in range(k + 1, 8):
                    below[q] = below[q] - m * s[q, k]
                acc = acc - m * r[k]
            row, part = r[k] * root, r[k] * inv[k]
            done = row if done is None else jnp.where(sub == k, row, done)
            mult = part if mult is None else jnp.where(sub == k, part, mult)
        out.append(jnp.where(lane <= sub + j0, done, 0.0))
        if g + 1 < groups:
            a[g + 1] = acc
        for t in near:
            c = side[t]
            new = jnp.where(inside, 0.0, a[t])
            for k in range(8):
                m = c[k] * inv[k]
                for q in range(k + 1, 8):
                    c[q] = c[q] - m * s[q, k]
                new = new - m * r[k]
            a[t] = new
        if g + 4 < groups:
            turned = mult.T
            for t in range(g + 4, groups):
                new = jnp.where(inside, 0.0, a[t])
                for k in range(8):
                    new = new - spread(turned[8 * t:8 * t + 8, :], k) * r[k]
                a[t] = new
        diag = ahead
        if g + 2 < groups:
            below = [spread(a[g + 2], j0 + 8 + q) for q in range(8)]
            ahead = [spread(a[g + 2], j0 + 16 + q) for q in range(8)]
    return jnp.concatenate(out, axis=0)


def factor(ext, inv, ybuf, arrive):
    for i in range(4):
        a, b = 128 * i, 128 * i + 128
        t = chol_inverse(ext[a:b, a:b])
        inv[i] = t
        if i == 0:
            arrive()
        y = nt(ybuf[:, a:b], t, HIGH)
        ybuf[:, a:b] = y
        if i < 3:
            low = nt(ext[b:512, a:b], t, HIGH)
            ext[b:512, a:b] = low
            ext[b:512, b:512] = ext[b:512, b:512] - nt(low, low, HIGH)
            ybuf[:, b:512] = ybuf[:, b:512] - nt(y, low, HIGH)


def solve(ext, inv, ybuf, zbuf, band):
    eye = jnp.where(lanes((128, 128)) == subs((128, 128)), 1.0, 0.0)
    for i in (3, 2, 1, 0):
        a, b = 128 * i, 128 * i + 128
        y = jnp.where(band < 4, jnp.where(band == i, -eye, 0.0), ybuf[:, a:b])
        if i < 3:
            y = y - nn(zbuf[:, b:512], ext[b:512, a:b])
        zbuf[:, a:b] = nn(y, inv[i])


NCH = 6
VLIM = 40 << 20
CH = 208


def filter_states(d, barrier_wait, v_ref, pot_ref, mass_ref, mat_ref, conn_ref, face_ref, own,
                  crow, frow, connb, faceb, potb, kp, amat, afac, bmat, gt, ft, gsel, v3, potc, potf, msk,
                  cnt, ws, wb, wf, ybuf, send, recv, vsend, vrecv, ssem, rsem, vsem, wgt):
    crow[...] = jnp.full(crow.shape, -1.0, f32)
    crow[0:1, 0:CELL] = conn_ref[0:1, :].astype(f32)
    crow[0:1, CP:CP + CELL] = conn_ref[1:2, :].astype(f32)
    frow[...] = jnp.full(frow.shape, -2.0, f32)
    frow[0:1, 0:FACE] = face_ref[0:1, :].astype(f32)
    for t in range(2):
        row = frow[0:1, 128 * t:128 * t + 128]
        faceb[128 * t:128 * t + 128, :] = jnp.broadcast_to(row, (128, 128)).T.astype(i32)
    potb[1152:1280, :] = jnp.zeros((128, 128), f32)
    v3[1216:ROWS, :] = jnp.zeros((ROWS - 1216, 512), bf16)
    for t in range(9):
        row = pot_ref[0:1, 128 * t:128 * t + 128]
        potb[128 * t:128 * t + 128, :] = jnp.broadcast_to(row, (128, 128)).T
    potb[OWNED - 128:OWNED, :] = jnp.broadcast_to(pot_ref[0:1, OWNED - 128:OWNED], (128, 128)).T
    hi, lo = split2(v_ref[...])
    v3[0:OWNED, 0:128] = hi
    v3[0:OWNED, 128:256] = lo
    hi, lo = split2(potb[0:OWNED, :])
    v3[0:OWNED, 256:384] = hi
    v3[0:OWNED, 384:512] = lo

    fsel = onehot(jnp.tile(faceb[0:FP, :], (1, ROWS // 128)) == lanes((FP, ROWS)))
    fv = dot(fsel, v3[...])
    vface = fv[:, 0:128] + fv[:, 128:256]
    potf[...] = fv[:, 256:384] + fv[:, 384:512]
    wf[0] = vface
    wf[1] = jnp.zeros((FP, COLS), f32)
    vsend[...] = vface.astype(bf16)
    ws[1] = jnp.zeros((CS, COLS), f32)
    barrier_wait()

    def vcopy(dst):
        return pltpu.make_async_remote_copy(
            src_ref=vsend, dst_ref=vrecv.at[pl.ds(0, FP), :], send_sem=vsem.at[0], recv_sem=vsem.at[1],
            device_id={"domain": dst}, device_id_type=MESHID)

    @pl.when(d > 0)
    def _():
        vcopy(d - 1).start()

    for t in range(CS // 128):
        row = crow[0:1, 128 * t:128 * t + 128]
        connb[128 * t:128 * t + 128, :] = jnp.broadcast_to(row, (128, 128)).T.astype(i32)
    kp[...] = jnp.zeros(kp.shape, bf16)
    kp[0:CELL, 0:CELL] = mat_ref[...]
    ci = crow[0:1, :].astype(i32)
    fi = frow[0:1, :].astype(i32)
    tup = onehot(subs((FP, CS), OWNED) == ci)
    tlo = onehot(jnp.tile(faceb[0:FP, :], (1, CS // 128)) == ci)
    both = jnp.concatenate([tup, tlo], axis=0)
    for c in range(2):
        cols = slice(CP * c, CP * c + CP)
        afac[:, cols] = dot(both[:, cols], kp[...]).astype(bf16)
    for t in range(ROWS // 128):
        gsel[:, 128 * t:128 * t + 128] = onehot(connb[...] == lanes((CS, 128), 128 * t))
    cv = dot(gsel[...], v3[...])
    ws[0] = cv[:, 0:128] + cv[:, 128:256]
    potc[...] = cv[:, 256:384] + cv[:, 384:512]
    cb2 = jnp.tile(connb[...], (1, 2))
    bmat[:, 0:256] = onehot(cb2 == fi)
    bmat[:, 256:512] = onehot(cb2 == lanes((CS, 256), OWNED))
    msk[...] = jnp.where((connb[...] >= OWNED) & (d == ND - 1), 0.0, 1.0)

    @pl.when(d < ND - 1)
    def _():
        vcopy(d).wait_recv()

    first = ws[0] + dot(bmat[:, 256:512], vrecv[...])
    ws[0] = first
    wb[...] = first.astype(bf16)

    def up(t, dst):
        return pltpu.make_async_remote_copy(
            src_ref=send.at[t, 0], dst_ref=recv.at[t, pl.ds(0, FP), :], send_sem=ssem.at[t, 0], recv_sem=rsem.at[t, 0],
            device_id={"domain": dst}, device_id_type=MESHID)

    def down(t, dst):
        return pltpu.make_async_remote_copy(
            src_ref=send.at[t, 1], dst_ref=recv.at[t, pl.ds(256, FP), :], send_sem=ssem.at[t, 1], recv_sem=rsem.at[t, 1],
            device_id={"domain": dst}, device_id_type=MESHID)

    def step(t, carry):
        now, then = lax.rem(t, 2), lax.rem(t + 1, 2)
        coef = jnp.where(t == 0, 0.125, 0.25).astype(f32)
        keep = jnp.where(t == 0, 0.0, 1.0).astype(f32)
        x = wb[...]
        send[t, 0] = dot(afac[0:FP, :], x).astype(bf16)

        @pl.when(d < ND - 1)
        def _():
            up(t, d + 1).start()

        wface = wf[now]
        lower = dot(afac[FP:2 * FP, :], x) + potf[...] * wface
        send[t, 1] = lower.astype(bf16)

        @pl.when(d > 0)
        def _():
            down(t, d - 1).start()

        @pl.when(t == 0)
        def _():
            km = kp[...]
            amat[0:CP, 0:CP] = km
            amat[CP:CS, CP:CS] = km
            none = jnp.zeros((CP, CP), bf16)
            c0 = jnp.tile(connb[0:CP, :], (1, CP // 128))
            e01 = jnp.where(c0 >= 0, onehot(c0 == crow[0:1, CP:CS].astype(i32)), none)
            amat[0:CP, CP:CS] = dot(e01, km).astype(bf16)
            c1 = jnp.tile(connb[CP:CS, :], (1, CP // 128))
            e10 = jnp.where(c1 >= 0, onehot(c1 == crow[0:1, 0:CP].astype(i32)), none)
            amat[CP:CS, 0:CP] = dot(e10, km).astype(bf16)

        ybuf[...] = dot(amat[...], x)

        @pl.when(t < 5)
        def _():
            at = pl.ds(pl.multiple_of(256 * t, 256), 256)
            g = onehot(subs((256, CS), 256 * t) == ci)
            h = onehot(subs((256, 256), 256 * t) == fi)
            gt[at, :] = g
            ft[at, :] = h
            cnt[at, :] = dot(g, jnp.ones((CS, COLS), bf16)) + dot(h, jnp.ones((256, COLS), bf16))

        @pl.when(t == 5)
        def _():
            for s in range(9):
                row = mass_ref[0:1, 128 * s:128 * s + 128]
                wgt[128 * s:128 * s + 128, :] = jnp.broadcast_to(row, (128, 128)).T * (1.0 / (ND * OWNED))
            wgt[1152:ROWS, :] = jnp.zeros((ROWS - 1152, 128), f32)
            row = mass_ref[0:1, OWNED - 128:OWNED]
            wgt[OWNED - 128:OWNED, :] = jnp.broadcast_to(row, (128, 128)).T * (1.0 / (ND * OWNED))

        @pl.when(d > 0)
        def _():
            up(t, d).wait_recv()
            down(t, d).wait_send()

        @pl.when(d < ND - 1)
        def _():
            down(t, d).wait_recv()
            up(t, d).wait_send()

        got = recv[t]
        wf[then] = coef * (lower + got[0:FP].astype(f32) - 9.0 * wface) - keep * wf[then]
        total = (ybuf[...] + dot(bmat[...], got)) * msk[...]
        new = coef * (total + (potc[...] - 9.0) * ws[now]) - keep * ws[then]
        ws[then] = new
        wb[...] = new.astype(bf16)
        return carry

    lax.fori_loop(0, DEGREE, step, 0)

    @pl.when(d > 0)
    def _():
        vcopy(d).wait_send()

    hi, lo = split2(ws[DEGREE % 2])
    back = dot(gt[...], jnp.concatenate([hi, lo], axis=1))
    hi, lo = split2(wf[DEGREE % 2])
    pad = jnp.zeros((256 - FP, 256), bf16)
    fback = dot(ft[...], jnp.concatenate([jnp.concatenate([hi, lo], axis=1), pad], axis=0))
    summed = (back + fback)[0:OWNED]
    count = cnt[0:OWNED, :]
    x = (potb[0:OWNED, :] - 9.0) * 0.125
    x2 = x * x
    alone = ((32.0 * x2 - 48.0) * x2 + 18.0) * x2 - 1.0
    own[0:OWNED, :] = jnp.where(count > 0.5, (summed[:, 0:128] + summed[:, 128:256]) / jnp.maximum(count, 1.0), alone * v_ref[...])
    own[OWNED:ROWS, :] = jnp.zeros((ROWS - OWNED, COLS), f32)


def strip_of(band):
    x = band // 4
    return 4 * (2 * lax.rem(band // 2, 2) + x // 2) + lax.rem(x, 2) * 2 + lax.rem(band, 2)


def ortho(own_ref, out_ref, d, band, wgt, pan, wt, sbm, rsm, sbg, rsg, agg, agm, gbuf, stripbuf, ext, inv, ybuf, zbuf, wcol,
          asem_s, asem_r, bsem_s, bsem_r, csem_s, csem_r, dsem_s, dsem_r, fsem_s,
          rg_s, rg_r, rm_s, rm_r, gg_s, gg_r, gm_s, gm_r, gx_s, gx_r, gy_s, gy_r):
    x = band // 4
    yh = lax.rem(band // 2, 2)
    c = lax.rem(band, 2)
    mine = lax.rem(band, 4)

    def copy(src, dst, ss, rs, to):
        return pltpu.make_async_remote_copy(src_ref=src, dst_ref=dst, send_sem=ss, recv_sem=rs,
                                            device_id={"band": to}, device_id_type=MESHID)

    def part(block, h):
        return pan.at[block, pl.ds(pl.multiple_of(h * CH, 16), CH), :]

    def acopy(h, slot, to):
        return copy(part(mine, h), part(mine, h), asem_s.at[slot, h], asem_r.at[h], to)

    y_peer = x * 4 + (1 - yh) * 2 + c
    c_peer = x * 4 + yh * 2 + (1 - c)
    across = (1 - yh) * 2 + c

    @pl.when(x == 0)
    def _():
        pan[mine, 0:NCH * CH, :] = own_ref[0:NCH * CH, :].astype(bf16)
        for k in range(NCH):
            acopy(k, 0, band + 4).start()
            acopy((k + 3) % NCH, 1, band + 12).start()

    def order(k):
        return jnp.where(x == 3, (k + 3) % NCH, jnp.where(x == 2, (k % 2) * 3 + k // 2, k))

    def bcopy(h):
        return copy(part(mine, h), part(mine, h), bsem_s.at[h], bsem_r.at[h], y_peer)

    def ccopy(h):
        return copy(part(mine, h), part(mine, h), csem_s.at[h], csem_r.at[h], c_peer)

    def dcopy(h):
        return copy(part(across, h), part(across, h), dsem_s.at[h], dsem_r.at[h], c_peer)

    def fcopy(h, k, to):
        return copy(part(mine, h), part(mine, h), fsem_s.at[k], asem_r.at[h], to)

    for k in range(NCH):
        h = order(k)

        @pl.when(x > 0)
        def _():
            acopy(h, 0, band).wait_recv()

        if k < 3:
            @pl.when((x == 1) | (x == 3))
            def _():
                fcopy(h, k, mine + 8).start()
        bcopy(h).start()
        ccopy(h).start()

    for t in range(10):
        at = slice(128 * t, 128 * t + 128)
        hi, lo = split2((own_ref[at, :] * wgt[at, :]).T)
        wt[0:128, at] = hi
        wt[128:256, at] = lo

    for h in range(NCH):
        copy(part(mine, h), part(mine, h), csem_s.at[h], csem_r.at[h], c_peer).wait_recv()
    wcol[...] = pan[2 * yh + x // 2].astype(f32) * wgt[...]
    sub = pl.multiple_of((lax.rem(x, 2) * 2 + c) * 32, 32)
    for t in range(10):
        at = slice(128 * t, 128 * t + 128)
        ybuf[0:128, 0:128] = wcol[at, :].T
        hi, lo = split2(ybuf[pl.ds(sub, 32), 0:128])
        wt[256:288, at] = hi
        wt[288:320, at] = lo

    def rows(m):
        return pl.ds(pl.multiple_of(m * 8, 8), 8)

    def rm(p, src_rows, slot, ss, to):
        return pltpu.make_async_remote_copy(
            src_ref=sbm.at[p, rows(src_rows), :], dst_ref=rsm.at[p, slot], send_sem=rm_s.at[p, ss], recv_sem=rm_r.at[p, slot],
            device_id={"domain": to}, device_id_type=MESHID)

    def rg(src_rows, slot, ss, to):
        return pltpu.make_async_remote_copy(
            src_ref=sbg.at[rows(src_rows), :], dst_ref=rsg.at[slot], send_sem=rg_s.at[ss], recv_sem=rg_r.at[slot],
            device_id={"domain": to}, device_id_type=MESHID)

    def products(p, panel):
        both = jnp.concatenate([pan[2 * panel], pan[2 * panel + 1]], axis=1)
        r = dot(wt[...], both)
        sbm[p] = r[0:128] + r[128:256]
        stripbuf[:, pl.ds(pl.multiple_of(panel * 256, 256), 256)] = r[256:288] + r[288:320]

    products(0, yh)
    for k in range(1, ND):
        to = lax.rem(d + k, ND)
        rm(0, to, d, k, to).start()

    for k in range(NCH):
        h = order(k)
        copy(part(across, h), part(across, h), bsem_s.at[h], bsem_r.at[h], y_peer).wait_recv()
        dcopy(h).start()
    for h in range(NCH):
        copy(part(mine, h), part(mine, h), dsem_s.at[h], dsem_r.at[h], c_peer).wait_recv()

    products(1, 1 - yh)
    for m in range(ND):
        sbg[8 * m:8 * m + 8, :] = stripbuf[8 * (m % 4):8 * (m % 4) + 8, 128 * (m // 4):128 * (m // 4) + 128]
    for k in range(1, ND):
        to = lax.rem(d + k, ND)
        rg(to, d, k, to).start()
    for k in range(1, ND):
        to = lax.rem(d + k, ND)
        rm(1, to, d, k, to).start()
    rsg[d] = sbg[rows(d), :]
    rsm[0, d] = sbm[0, rows(d), :]
    rsm[1, d] = sbm[1, rows(d), :]
    for k in range(1, ND):
        frm = lax.rem(d + k, ND)
        rg(frm, frm, k, frm).wait_recv()
    total = rsg[0]
    for m in range(1, ND):
        total = total + rsg[m]
    agg[rows(d), :] = total

    def ag(buf, who, ss, rr, k, to):
        view = buf.at[rows(who), :]
        return pltpu.make_async_remote_copy(
            src_ref=view, dst_ref=view, send_sem=ss.at[k], recv_sem=rr.at[who],
            device_id={"domain": to}, device_id_type=MESHID)

    for k in range(1, ND):
        to = lax.rem(d + k, ND)
        ag(agg, d, gg_s, gg_r, k, to).start()
    for p in range(2):
        for k in range(1, ND):
            frm = lax.rem(d + k, ND)
            rm(p, frm, frm, k, frm).wait_recv()
        total = rsm[p, 0]
        for m in range(1, ND):
            total = total + rsm[p, m]
        panel = yh if p == 0 else 1 - yh
        agm[rows(d), pl.ds(pl.multiple_of(panel * 256, 256), 256)] = total
    for k in range(1, ND):
        frm = lax.rem(d + k, ND)
        ag(agg, frm, gg_s, gg_r, k, frm).wait_recv()

    here = strip_of(band)
    gbuf[here] = agg[...]
    chip = band // 2

    def row_of(b):
        return 2 * lax.rem(b // 2, 2) + b // 8

    def strip(who, q, ss, rr, k, to):
        view = gbuf.at[who, pl.ds(32 * q, 32), :]
        return copy(view, view, ss.at[k, q], rr.at[who, q], to)

    def blocks(b, act):
        for q in range(4):
            if q == 3:
                act(q)
            else:
                pl.when(row_of(b) <= q)(functools.partial(act, q))

    for k in range(1, 8):
        to = lax.rem(chip + k, 8) * 2 + c
        blocks(band, lambda q: strip(here, q, gx_s, gx_r, k, to).start())
    blocks(band, lambda q: strip(here, q, gy_s, gy_r, 0, c_peer).start())
    for k in range(1, ND):
        to = lax.rem(d + k, ND)
        ag(agm, d, gm_s, gm_r, k, to).start()
    for k in range(1, 8):
        who = lax.rem(chip + k, 8) * 2 + c
        frm = strip_of(who)

        def relay(q):
            strip(frm, q, gx_s, gx_r, k, c_peer).wait_recv()
            strip(frm, q, gy_s, gy_r, k, c_peer).start()

        blocks(who, relay)
    for k in range(8):
        who = lax.rem(chip + k, 8) * 2 + (1 - c)
        frm = strip_of(who)
        blocks(who, lambda q: strip(frm, q, gy_s, gy_r, k, c_peer).wait_recv())

    for b in range(16):
        for m in range(ND):
            if m // 4 >= b // 4:
                ext[32 * b + 8 * (m % 4):32 * b + 8 * (m % 4) + 8, 128 * (m // 4):128 * (m // 4) + 128] = gbuf[b, 8 * m:8 * m + 8, :]
    for i in range(3):
        for j in range(i + 1, 4):
            ext[128 * j:128 * j + 128, 128 * i:128 * i + 128] = ext[128 * i:128 * i + 128, 128 * j:128 * j + 128].T

    def arrive():
        for k in range(1, ND):
            frm = lax.rem(d + k, ND)
            ag(agm, frm, gm_s, gm_r, k, frm).wait_recv()
        ybuf[...] = agm[...]

    factor(ext, inv, ybuf, arrive)
    solve(ext, inv, ybuf, zbuf, band)

    own = own_ref[0:OWNED, :]
    zh, zl = split2(zbuf[...])
    zz = jnp.concatenate([zh, zl], axis=0)
    pair = [jnp.concatenate([pan[0], pan[1]], axis=1), jnp.concatenate([pan[2], pan[3]], axis=1)]
    prod = nt(pair[0], zz[:, 0:256]) + nt(pair[1], zz[:, 256:512])
    update = prod[0:OWNED, 0:128] + prod[0:OWNED, 128:256]
    is_panel = band < 4
    zown = zbuf[:, pl.ds(pl.multiple_of(jnp.minimum(band, 3) * 128, 128), 128)]
    rest = (own - own.astype(bf16).astype(f32)).astype(bf16)
    fix = nt(rest, zown.astype(bf16))
    out_ref[...] = jnp.where(is_panel, -update - fix, own - update)

    @pl.when(x == 0)
    def _():
        for h in range(NCH):
            acopy(h, 0, y_peer).wait_send()
            acopy(h, 1, y_peer).wait_send()

    @pl.when((x == 1) | (x == 3))
    def _():
        for k in range(3):
            fcopy(0, k, y_peer).wait_send()

    for h in range(NCH):
        bcopy(h).wait_send()
        ccopy(h).wait_send()
        dcopy(h).wait_send()
    for k in range(1, ND):
        to = lax.rem(d + k, ND)
        rg(d, d, k, to).wait_send()
        rm(0, d, d, k, to).wait_send()
        rm(1, d, d, k, to).wait_send()
        ag(agg, d, gg_s, gg_r, k, to).wait_send()
        ag(agm, d, gm_s, gm_r, k, to).wait_send()
    for k in range(1, 8):
        blocks(band, lambda q: strip(here, q, gx_s, gx_r, k, c_peer).wait_send())
    blocks(band, lambda q: strip(here, q, gy_s, gy_r, 0, c_peer).wait_send())
    for k in range(1, 8):
        blocks(lax.rem(chip + k, 8) * 2 + c, lambda q: strip(here, q, gy_s, gy_r, k, c_peer).wait_send())


def kernel(v_hbm, pot_hbm, mass_hbm, mat_hbm, conn_hbm, face_hbm, out_ref, v_ref, pot_ref, mass_ref, mat_ref, conn_ref, face_ref, isem, own, wgt, vrecv, recv, pan, pot_row, mass_row, *scratch):
    d = lax.axis_index("domain")
    band = lax.axis_index("band")
    loads = [pltpu.make_async_copy(src, dst, isem.at[k]) for k, (src, dst) in enumerate((
        (face_hbm, face_ref), (pot_hbm, pot_ref), (v_hbm, v_ref), (conn_hbm, conn_ref), (mat_hbm, mat_ref), (mass_hbm, mass_ref)))]
    for load in loads:
        load.start()
    vrecv[...] = jnp.zeros(vrecv.shape, bf16)
    recv[...] = jnp.zeros(recv.shape, bf16)
    for j in range(4):
        pan[j, NCH * CH:ROWS, :] = jnp.zeros((ROWS - NCH * CH, COLS), bf16)
    barrier = pltpu.get_barrier_semaphore()
    for k in range(1, 16):
        pl.semaphore_signal(barrier, inc=1, device_id={"domain": lax.rem(d + k, ND)}, device_id_type=MESHID)
        pl.semaphore_signal(barrier, inc=1, device_id={"band": lax.rem(band + k, 16)}, device_id_type=MESHID)
    for load in loads[:4]:
        load.wait()
    pot_row[...] = pot_ref[...].reshape(1, OWNED)
    n = len(FILTER)
    f = scratch[:n]

    def barrier_wait():
        pl.semaphore_wait(barrier, 30)
        loads[4].wait()
        loads[5].wait()
        mass_row[...] = mass_ref[...].reshape(1, OWNED)

    filter_states(d, barrier_wait, v_ref, pot_row, mass_row, mat_ref, conn_ref, face_ref, own,
                  *f[:22], recv, f[22], vrecv, *f[23:], wgt)
    ortho(own, out_ref, d, band, wgt, pan, *scratch[n:])


V = pltpu.VMEM
D = pltpu.SemaphoreType.DMA
FILTER = (
    V((8, CS), f32), V((8, 256), f32), V((CS, 128), i32), V((256, 128), i32), V((ROWS, 128), f32),
    V((CP, CP), bf16), V((CS, CS), bf16), V((2 * FP, CS), bf16), V((CS, 512), bf16), V((ROWS, CS), bf16),
    V((ROWS, 256), bf16), V((CS, ROWS), bf16), V((ROWS, 512), bf16), V((CS, 128), f32), V((FP, 128), f32),
    V((CS, 128), f32), V((ROWS, 128), f32), V((2, CS, COLS), f32), V((CS, COLS), bf16), V((2, FP, COLS), f32),
    V((CS, COLS), f32),
    V((DEGREE, 2, FP, COLS), bf16), V((FP, COLS), bf16),
    D((DEGREE, 2)), D((DEGREE, 2)), D((2,)),
)
ORTHO = (
    V((320, ROWS), bf16), V((2, 128, 256), f32), V((2, ND, 8, 256), f32), V((128, 128), f32), V((ND, 8, 128), f32),
    V((128, 128), f32), V((128, 512), f32), V((16, 128, 128), f32), V((32, 512), f32), V((512, 512), f32), V((4, 128, 128), f32),
    V((128, 512), f32), V((128, 512), f32), V((ROWS, COLS), f32),
    D((2, NCH)), D((NCH,)), D((NCH,)), D((NCH,)), D((NCH,)), D((NCH,)), D((NCH,)), D((NCH,)), D((3,)),
    D((ND,)), D((ND,)), D((2, ND)), D((2, ND)), D((ND,)), D((ND,)), D((ND,)), D((ND,)), D((8, 4)), D((16, 4)), D((8, 4)), D((16, 4)),
)
SHARED = (V((OWNED, COLS), f32), V((OWNED,), f32), V((OWNED,), f32), V((CELL, CELL), bf16), V((2, CELL), i32), V((1, FACE), i32), D((6,)),
          V((ROWS, COLS), f32), V((ROWS, 128), f32), V((256, COLS), bf16), V((DEGREE, 512, COLS), bf16), V((4, ROWS, COLS), bf16), V((1, OWNED), f32), V((1, OWNED), f32))


def per_device(states, potential, node_mass, cell_matrix, connectivity, face_rows):
    return pl.pallas_call(
        kernel,
        out_shape=jax.ShapeDtypeStruct((OWNED, COLS), f32),
        in_specs=[pl.BlockSpec(memory_space=pltpu.HBM)] * 6,
        out_specs=VM,
        scratch_shapes=list(SHARED + FILTER + ORTHO),
        compiler_params=pltpu.CompilerParams(collective_id=0, has_side_effects=True, vmem_limit_bytes=VLIM),
        name="subspace",
    )(states, potential, node_mass, cell_matrix, connectivity, face_rows)


def solution(mesh):
    return jax.shard_map(
        per_device, mesh=mesh,
        in_specs=(P("domain", "band"), P("domain"), P("domain"), P(), P("domain", None), P("domain", None)),
        out_specs=P("domain", "band"), check_vma=False,
    )
```

```python
import functools
import jax
import jax.numpy as jnp
from jax import lax
from jax.experimental import pallas as pl
from jax.experimental.pallas import tpu as pltpu
from jax.sharding import PartitionSpec as P

f32 = jnp.float32
bf16 = jnp.bfloat16
i32 = jnp.int32
OWNED = 1224
ROWS = 1280
CELL = 729
CP = 768
CS = 1536
FACE = 153
FP = 160
COLS = 128
DEGREE = 6
ND = 16
MESHID = pl.DeviceIdType.MESH
VM = pl.BlockSpec(memory_space=pltpu.VMEM)


def dot(a, b):
    return jnp.dot(a, b, preferred_element_type=f32)


def split2(x):
    hi = x.astype(bf16)
    return hi, (x - hi.astype(f32)).astype(bf16)


def split3(x):
    hi = x.astype(bf16)
    rest = x - hi.astype(f32)
    mid = rest.astype(bf16)
    return hi, mid, (rest - mid.astype(f32)).astype(bf16)


def lanes(shape, base=0):
    return lax.broadcasted_iota(i32, shape, 1) + base


def subs(shape, base=0):
    return lax.broadcasted_iota(i32, shape, 0) + base


def onehot(mask):
    return jnp.where(mask, 1.0, 0.0).astype(bf16)


HIGH = lax.Precision.HIGHEST


def nt(a, b, precision=None):
    return lax.dot_general(a, b, (((1,), (1,)), ((), ())), preferred_element_type=f32, precision=precision)


def nn(a, b):
    return jnp.dot(a, b, preferred_element_type=f32, precision=HIGH)


def chol_inverse(block):
    n, groups = 128, 16
    shape = (8, n)
    lane = lanes(shape)
    sub = subs(shape)

    def spread(x, j):
        return jnp.broadcast_to(x[:, j:j + 1], shape)

    def pick(x, i):
        return jnp.take_along_axis(x, jnp.full(shape, i, i32), axis=0)

    a = [block[8 * k:8 * k + 8, :] for k in range(groups)]
    out = []
    diag = [spread(a[0], q) for q in range(8)]
    below = [spread(a[1], q) for q in range(8)]
    ahead = [spread(a[1], 8 + q) for q in range(8)]
    for g in range(groups):
        j0 = 8 * g
        inside = (lane >= j0) & (lane < j0 + 8)
        s = {(i, k): pick(diag[k], i) for k in range(8) for i in range(k, 8)}
        r = [jnp.where(inside, 0.0, pick(a[g], i)) for i in range(8)]
        near = range(g + 2, min(g + 4, groups))
        side = {t: [spread(a[t], j0 + k) for k in range(8)] for t in near}
        inv, done, mult = [], None, None
        acc = jnp.where(inside, 0.0, a[g + 1]) if g + 1 < groups else None
        for k in range(8):
            root = lax.rsqrt(s[k, k])
            inv.append(root * root)
            r[k] = jnp.where(lane == j0 + k, 1.0, r[k])
            for i in range(k + 1, 8):
                m = s[i, k] * inv[k]
                for q in range(k + 1, i + 1):
                    s[i, q] = s[i, q] - m * s[q, k]
                r[i] = r[i] - m * r[k]
            if g + 1 < groups:
                m = below[k] * inv[k]
                for q in range(8):
                    ahead[q] = ahead[q] - m * pick(below[k], q)
                for q in range(k + 1, 8):
                    below[q] = below[q] - m * s[q, k]
                acc = acc - m * r[k]
            row, part = r[k] * root, r[k] * inv[k]
            done = row if done is None else jnp.where(sub == k, row, done)
            mult = part if mult is None else jnp.where(sub == k, part, mult)
        out.append(jnp.where(lane <= sub + j0, done, 0.0))
        if g + 1 < groups:
            a[g + 1] = acc
        for t in near:
            c = side[t]
            new = jnp.where(inside, 0.0, a[t])
            for k in range(8):
                m = c[k] * inv[k]
                for q in range(k + 1, 8):
                    c[q] = c[q] - m * s[q, k]
                new = new - m * r[k]
            a[t] = new
        if g + 4 < groups:
            turned = mult.T
            for t in range(g + 4, groups):
                new = jnp.where(inside, 0.0, a[t])
                for k in range(8):
                    new = new - spread(turned[8 * t:8 * t + 8, :], k) * r[k]
                a[t] = new
        diag = ahead
        if g + 2 < groups:
            below = [spread(a[g + 2], j0 + 8 + q) for q in range(8)]
            ahead = [spread(a[g + 2], j0 + 16 + q) for q in range(8)]
    return jnp.concatenate(out, axis=0)


def nt3(a, b):
    ah, al = split2(a)
    bh, bl = split2(b)
    return nt(jnp.concatenate([ah, ah, al], axis=1), jnp.concatenate([bh, bl, bh], axis=1))


def nn3(a, b):
    ah, al = split2(a)
    bh, bl = split2(b)
    return dot(jnp.concatenate([ah, ah, al], axis=1), jnp.concatenate([bh, bl, bh], axis=0))


def factor(ext, inv, ybuf, arrive):
    def forward(i):
        a, b = 128 * i, 128 * i + 128
        y = nt3(ybuf[:, a:b], inv[i])
        ybuf[:, a:b] = y
        if i < 3:
            ybuf[:, b:512] = ybuf[:, b:512] - nt3(y, ext[b:512, a:b])

    for i in range(4):
        a, b = 128 * i, 128 * i + 128
        t = chol_inverse(ext[a:b, a:b])
        inv[i] = t
        if i < 3:
            low = nt3(ext[b:512, a:b], t)
            ext[b:512, a:b] = low
            ext[b:512, b:512] = ext[b:512, b:512] - nt3(low, low)
        if i == 1:
            arrive()
            forward(0)
        if i > 0:
            forward(i)


def solve(ext, inv, ybuf, zbuf, band):
    eye = jnp.where(lanes((128, 128)) == subs((128, 128)), 1.0, 0.0)
    for i in (3, 2, 1, 0):
        a, b = 128 * i, 128 * i + 128
        y = jnp.where(band < 4, jnp.where(band == i, -eye, 0.0), ybuf[:, a:b])
        if i < 3:
            y = y - nn3(zbuf[:, b:512], ext[b:512, a:b])
        zbuf[:, a:b] = nn3(y, inv[i])


NCH = 6
VLIM = 60 << 20
CH = 208


def filter_states(d, barrier_wait, v_ref, pot_ref, mass_ref, mat_ref, conn_ref, face_ref, own,
                  crow, frow, connb, faceb, potb, kp, amat, afac, bmat, gt, ft, gsel, v3, potc, potf, msk,
                  cnt, ws, wb, wf, ybuf, send, recv, vsend, vrecv, ssem, rsem, vsem, wgt):
    crow[...] = jnp.full(crow.shape, -1.0, f32)
    crow[0:1, 0:CELL] = conn_ref[0:1, :].astype(f32)
    crow[0:1, CP:CP + CELL] = conn_ref[1:2, :].astype(f32)
    frow[...] = jnp.full(frow.shape, -2.0, f32)
    frow[0:1, 0:FACE] = face_ref[0:1, :].astype(f32)
    for t in range(2):
        row = frow[0:1, 128 * t:128 * t + 128]
        faceb[128 * t:128 * t + 128, :] = jnp.broadcast_to(row, (128, 128)).T.astype(i32)
    potb[1152:1280, :] = jnp.zeros((128, 128), f32)
    v3[1216:ROWS, :] = jnp.zeros((ROWS - 1216, 512), bf16)
    for t in range(9):
        row = pot_ref[0:1, 128 * t:128 * t + 128]
        potb[128 * t:128 * t + 128, :] = jnp.broadcast_to(row, (128, 128)).T
    potb[OWNED - 128:OWNED, :] = jnp.broadcast_to(pot_ref[0:1, OWNED - 128:OWNED], (128, 128)).T
    hi, lo = split2(v_ref[...])
    v3[0:OWNED, 0:128] = hi
    v3[0:OWNED, 128:256] = lo
    hi, lo = split2(potb[0:OWNED, :])
    v3[0:OWNED, 256:384] = hi
    v3[0:OWNED, 384:512] = lo

    fsel = onehot(jnp.tile(faceb[0:FP, :], (1, ROWS // 128)) == lanes((FP, ROWS)))
    fv = dot(fsel, v3[...])
    vface = fv[:, 0:128] + fv[:, 128:256]
    potf[...] = fv[:, 256:384] + fv[:, 384:512]
    wf[0] = vface
    wf[1] = jnp.zeros((FP, COLS), f32)
    vsend[...] = vface.astype(bf16)
    ws[1] = jnp.zeros((CS, COLS), f32)
    barrier_wait()

    def vcopy(dst):
        return pltpu.make_async_remote_copy(
            src_ref=vsend, dst_ref=vrecv.at[pl.ds(0, FP), :], send_sem=vsem.at[0], recv_sem=vsem.at[1],
            device_id={"domain": dst}, device_id_type=MESHID)

    @pl.when(d > 0)
    def _():
        vcopy(d - 1).start()

    for t in range(CS // 128):
        row = crow[0:1, 128 * t:128 * t + 128]
        connb[128 * t:128 * t + 128, :] = jnp.broadcast_to(row, (128, 128)).T.astype(i32)
    kp[...] = jnp.zeros(kp.shape, bf16)
    kp[0:CELL, 0:CELL] = mat_ref[...]
    ci = crow[0:1, :].astype(i32)
    fi = frow[0:1, :].astype(i32)
    tup = onehot(subs((FP, CS), OWNED) == ci)
    tlo = onehot(jnp.tile(faceb[0:FP, :], (1, CS // 128)) == ci)
    both = jnp.concatenate([tup, tlo], axis=0)
    for c in range(2):
        cols = slice(CP * c, CP * c + CP)
        afac[:, cols] = dot(both[:, cols], kp[...]).astype(bf16)
    for t in range(ROWS // 128):
        gsel[:, 128 * t:128 * t + 128] = onehot(connb[...] == lanes((CS, 128), 128 * t))
    cv = dot(gsel[...], v3[...])
    ws[0] = cv[:, 0:128] + cv[:, 128:256]
    potc[...] = cv[:, 256:384] + cv[:, 384:512]
    cb2 = jnp.tile(connb[...], (1, 2))
    bmat[:, 0:256] = onehot(cb2 == fi)
    bmat[:, 256:512] = onehot(cb2 == lanes((CS, 256), OWNED))
    msk[...] = jnp.where((connb[...] >= OWNED) & (d == ND - 1), 0.0, 1.0)

    @pl.when(d < ND - 1)
    def _():
        vcopy(d).wait_recv()

    first = ws[0] + dot(bmat[:, 256:512], vrecv[...])
    ws[0] = first
    wb[...] = first.astype(bf16)

    def up(t, dst):
        return pltpu.make_async_remote_copy(
            src_ref=send.at[t, 0], dst_ref=recv.at[t, pl.ds(0, FP), :], send_sem=ssem.at[t, 0], recv_sem=rsem.at[t, 0],
            device_id={"domain": dst}, device_id_type=MESHID)

    def down(t, dst):
        return pltpu.make_async_remote_copy(
            src_ref=send.at[t, 1], dst_ref=recv.at[t, pl.ds(256, FP), :], send_sem=ssem.at[t, 1], recv_sem=rsem.at[t, 1],
            device_id={"domain": dst}, device_id_type=MESHID)

    def step(t, carry):
        now, then = lax.rem(t, 2), lax.rem(t + 1, 2)
        coef = jnp.where(t == 0, 0.125, 0.25).astype(f32)
        keep = jnp.where(t == 0, 0.0, 1.0).astype(f32)
        x = wb[...]
        send[t, 0] = dot(afac[0:FP, :], x).astype(bf16)

        @pl.when(d < ND - 1)
        def _():
            up(t, d + 1).start()

        wface = wf[now]
        lower = dot(afac[FP:2 * FP, :], x) + potf[...] * wface
        send[t, 1] = lower.astype(bf16)

        @pl.when(d > 0)
        def _():
            down(t, d - 1).start()

        @pl.when(t == 0)
        def _():
            km = kp[...]
            amat[0:CP, 0:CP] = km
            amat[CP:CS, CP:CS] = km
            none = jnp.zeros((CP, CP), bf16)
            c0 = jnp.tile(connb[0:CP, :], (1, CP // 128))
            e01 = jnp.where(c0 >= 0, onehot(c0 == crow[0:1, CP:CS].astype(i32)), none)
            amat[0:CP, CP:CS] = dot(e01, km).astype(bf16)
            c1 = jnp.tile(connb[CP:CS, :], (1, CP // 128))
            e10 = jnp.where(c1 >= 0, onehot(c1 == crow[0:1, 0:CP].astype(i32)), none)
            amat[CP:CS, 0:CP] = dot(e10, km).astype(bf16)

        ybuf[...] = coef * (dot(amat[...], x) * msk[...] + (potc[...] - 9.0) * ws[now]) - keep * ws[then]

        @pl.when(t < 5)
        def _():
            at = pl.ds(pl.multiple_of(256 * t, 256), 256)
            g = onehot(subs((256, CS), 256 * t) == ci)
            h = onehot(subs((256, 256), 256 * t) == fi)
            gt[at, :] = g
            ft[at, :] = h
            cnt[at, :] = dot(g, jnp.ones((CS, COLS), bf16)) + dot(h, jnp.ones((256, COLS), bf16))

        @pl.when(t == 5)
        def _():
            for s in range(9):
                row = mass_ref[0:1, 128 * s:128 * s + 128]
                wgt[128 * s:128 * s + 128, :] = jnp.broadcast_to(row, (128, 128)).T * (1.0 / (ND * OWNED))
            wgt[1152:ROWS, :] = jnp.zeros((ROWS - 1152, 128), f32)
            row = mass_ref[0:1, OWNED - 128:OWNED]
            wgt[OWNED - 128:OWNED, :] = jnp.broadcast_to(row, (128, 128)).T * (1.0 / (ND * OWNED))

        @pl.when(d > 0)
        def _():
            up(t, d).wait_recv()

        @pl.when(d < ND - 1)
        def _():
            down(t, d).wait_recv()

        got = recv[t]
        wf[then] = coef * (lower + got[0:FP].astype(f32) - 9.0 * wface) - keep * wf[then]
        new = ybuf[...] + coef * dot(bmat[...], got)
        ws[then] = new
        wb[...] = new.astype(bf16)
        return carry

    lax.fori_loop(0, DEGREE, step, 0)

    @pl.when(d > 0)
    def _():
        vcopy(d).wait_send()
        for t in range(DEGREE):
            down(t, d).wait_send()

    @pl.when(d < ND - 1)
    def _():
        for t in range(DEGREE):
            up(t, d).wait_send()

    hi, lo = split2(ws[DEGREE % 2])
    back = dot(gt[...], jnp.concatenate([hi, lo], axis=1))
    hi, lo = split2(wf[DEGREE % 2])
    pad = jnp.zeros((256 - FP, 256), bf16)
    fback = dot(ft[...], jnp.concatenate([jnp.concatenate([hi, lo], axis=1), pad], axis=0))
    summed = (back + fback)[0:OWNED]
    count = cnt[0:OWNED, :]
    x = (potb[0:OWNED, :] - 9.0) * 0.125
    x2 = x * x
    alone = ((32.0 * x2 - 48.0) * x2 + 18.0) * x2 - 1.0
    own[0:OWNED, :] = jnp.where(count > 0.5, (summed[:, 0:128] + summed[:, 128:256]) / jnp.maximum(count, 1.0), alone * v_ref[...])
    own[OWNED:ROWS, :] = jnp.zeros((ROWS - OWNED, COLS), f32)


def strip_of(band):
    x = band // 4
    return 4 * (2 * lax.rem(band // 2, 2) + x // 2) + lax.rem(x, 2) * 2 + lax.rem(band, 2)


def ortho(own_ref, out_ref, d, band, wgt, pan, wt, sbm, rsm, sbg, rsg, agg, agm, gbuf, stripbuf, ext, inv, ybuf, zbuf, wcol,
          asem_s, asem_r, bsem_s, bsem_r, csem_s, csem_r, dsem_s, dsem_r, fsem_s,
          rg_s, rg_r, rm_s, rm_r, gg_s, gg_r, gm_s, gm_r, gx_s, gx_r, gy_s, gy_r):
    x = band // 4
    yh = lax.rem(band // 2, 2)
    c = lax.rem(band, 2)
    mine = lax.rem(band, 4)

    def copy(src, dst, ss, rs, to):
        return pltpu.make_async_remote_copy(src_ref=src, dst_ref=dst, send_sem=ss, recv_sem=rs,
                                            device_id={"band": to}, device_id_type=MESHID)

    def part(block, h):
        return pan.at[block, pl.ds(pl.multiple_of(h * CH, 16), CH), :]

    def acopy(h, slot, to):
        return copy(part(mine, h), part(mine, h), asem_s.at[slot, h], asem_r.at[h], to)

    y_peer = x * 4 + (1 - yh) * 2 + c
    c_peer = x * 4 + yh * 2 + (1 - c)
    across = (1 - yh) * 2 + c

    @pl.when(x == 0)
    def _():
        pan[mine, 0:NCH * CH, :] = own_ref[0:NCH * CH, :].astype(bf16)
        for k in range(NCH):
            acopy(k, 0, band + 4).start()
            acopy((k + 3) % NCH, 1, band + 12).start()

    def order(k):
        return jnp.where(x == 3, (k + 3) % NCH, jnp.where(x == 2, (k % 2) * 3 + k // 2, k))

    def bcopy(h):
        return copy(part(mine, h), part(mine, h), bsem_s.at[h], bsem_r.at[h], y_peer)

    def ccopy(h):
        return copy(part(mine, h), part(mine, h), csem_s.at[h], csem_r.at[h], c_peer)

    def dcopy(h):
        return copy(part(across, h), part(across, h), dsem_s.at[h], dsem_r.at[h], c_peer)

    def fcopy(h, k, to):
        return copy(part(mine, h), part(mine, h), fsem_s.at[k], asem_r.at[h], to)

    for k in range(NCH):
        h = order(k)

        @pl.when(x > 0)
        def _():
            acopy(h, 0, band).wait_recv()

        if k < 3:
            @pl.when((x == 1) | (x == 3))
            def _():
                fcopy(h, k, mine + 8).start()
        bcopy(h).start()
        ccopy(h).start()

    for t in range(10):
        at = slice(128 * t, 128 * t + 128)
        hi, lo = split2((own_ref[at, :] * wgt[at, :]).T)
        wt[0:128, at] = hi
        wt[128:256, at] = lo

    for h in range(NCH):
        copy(part(mine, h), part(mine, h), csem_s.at[h], csem_r.at[h], c_peer).wait_recv()
    wcol[...] = pan[2 * yh + x // 2].astype(f32) * wgt[...]
    sub = pl.multiple_of((lax.rem(x, 2) * 2 + c) * 32, 32)
    for t in range(10):
        at = slice(128 * t, 128 * t + 128)
        ybuf[0:128, 0:128] = wcol[at, :].T
        hi, lo = split2(ybuf[pl.ds(sub, 32), 0:128])
        wt[256:288, at] = hi
        wt[288:320, at] = lo

    def rows(m):
        return pl.ds(pl.multiple_of(m * 8, 8), 8)

    def rm(p, src_rows, slot, ss, to):
        return pltpu.make_async_remote_copy(
            src_ref=sbm.at[p, rows(src_rows), :], dst_ref=rsm.at[p, slot], send_sem=rm_s.at[p, ss], recv_sem=rm_r.at[p, slot],
            device_id={"domain": to}, device_id_type=MESHID)

    def rg(src_rows, slot, ss, to):
        return pltpu.make_async_remote_copy(
            src_ref=sbg.at[rows(src_rows), :], dst_ref=rsg.at[slot], send_sem=rg_s.at[ss], recv_sem=rg_r.at[slot],
            device_id={"domain": to}, device_id_type=MESHID)

    def products(p, panel):
        both = jnp.concatenate([pan[2 * panel], pan[2 * panel + 1]], axis=1)
        r = dot(wt[...], both)
        sbm[p] = r[0:128] + r[128:256]
        stripbuf[:, pl.ds(pl.multiple_of(panel * 256, 256), 256)] = r[256:288] + r[288:320]

    products(0, yh)
    for k in range(1, ND):
        to = lax.rem(d + k, ND)
        rm(0, to, d, k, to).start()

    for k in range(NCH):
        h = order(k)
        copy(part(across, h), part(across, h), bsem_s.at[h], bsem_r.at[h], y_peer).wait_recv()
        dcopy(h).start()
    for h in range(NCH):
        copy(part(mine, h), part(mine, h), dsem_s.at[h], dsem_r.at[h], c_peer).wait_recv()

    products(1, 1 - yh)
    for m in range(ND):
        sbg[8 * m:8 * m + 8, :] = stripbuf[8 * (m % 4):8 * (m % 4) + 8, 128 * (m // 4):128 * (m // 4) + 128]
    for k in range(1, ND):
        to = lax.rem(d + k, ND)
        rg(to, d, k, to).start()
    for k in range(1, ND):
        to = lax.rem(d + k, ND)
        rm(1, to, d, k, to).start()
    rsg[d] = sbg[rows(d), :]
    rsm[0, d] = sbm[0, rows(d), :]
    rsm[1, d] = sbm[1, rows(d), :]
    for k in range(1, ND):
        frm = lax.rem(d + k, ND)
        rg(frm, frm, k, frm).wait_recv()
    total = rsg[0]
    for m in range(1, ND):
        total = total + rsg[m]
    agg[rows(d), :] = total

    def ag(buf, who, ss, rr, k, to):
        view = buf.at[rows(who), :]
        return pltpu.make_async_remote_copy(
            src_ref=view, dst_ref=view, send_sem=ss.at[k], recv_sem=rr.at[who],
            device_id={"domain": to}, device_id_type=MESHID)

    for k in range(1, ND):
        to = lax.rem(d + k, ND)
        ag(agg, d, gg_s, gg_r, k, to).start()
    for k in range(1, ND):
        frm = lax.rem(d + k, ND)
        ag(agg, frm, gg_s, gg_r, k, frm).wait_recv()

    here = strip_of(band)
    gbuf[here] = agg[...]
    chip = band // 2

    def row_of(b):
        return 2 * lax.rem(b // 2, 2) + b // 8

    def strip(who, q, ss, rr, k, to):
        view = gbuf.at[who, pl.ds(32 * q, 32), :]
        return copy(view, view, ss.at[k, q], rr.at[who, q], to)

    def blocks(b, act):
        for q in range(4):
            if q == 3:
                act(q)
            else:
                pl.when(row_of(b) <= q)(functools.partial(act, q))

    for k in range(1, 8):
        to = lax.rem(chip + k, 8) * 2 + c
        blocks(band, lambda q: strip(here, q, gx_s, gx_r, k, to).start())
    blocks(band, lambda q: strip(here, q, gy_s, gy_r, 0, c_peer).start())
    for p in range(2):
        for k in range(1, ND):
            frm = lax.rem(d + k, ND)
            rm(p, frm, frm, k, frm).wait_recv()
        total = rsm[p, 0]
        for m in range(1, ND):
            total = total + rsm[p, m]
        panel = yh if p == 0 else 1 - yh
        agm[rows(d), pl.ds(pl.multiple_of(panel * 256, 256), 256)] = total
    for k in range(1, ND):
        to = lax.rem(d + k, ND)
        ag(agm, d, gm_s, gm_r, k, to).start()
    for k in range(1, 8):
        who = lax.rem(chip + k, 8) * 2 + c
        frm = strip_of(who)

        def relay(q):
            strip(frm, q, gx_s, gx_r, k, c_peer).wait_recv()
            strip(frm, q, gy_s, gy_r, k, c_peer).start()

        blocks(who, relay)
    for k in range(8):
        who = lax.rem(chip + k, 8) * 2 + (1 - c)
        frm = strip_of(who)
        blocks(who, lambda q: strip(frm, q, gy_s, gy_r, k, c_peer).wait_recv())

    for b in range(16):
        for m in range(ND):
            if m // 4 >= b // 4:
                ext[32 * b + 8 * (m % 4):32 * b + 8 * (m % 4) + 8, 128 * (m // 4):128 * (m // 4) + 128] = gbuf[b, 8 * m:8 * m + 8, :]
    for i in range(3):
        for j in range(i + 1, 4):
            ext[128 * j:128 * j + 128, 128 * i:128 * i + 128] = ext[128 * i:128 * i + 128, 128 * j:128 * j + 128].T

    def arrive():
        for k in range(1, ND):
            frm = lax.rem(d + k, ND)
            ag(agm, frm, gm_s, gm_r, k, frm).wait_recv()
        ybuf[...] = agm[...]

    factor(ext, inv, ybuf, arrive)
    solve(ext, inv, ybuf, zbuf, band)

    own = own_ref[0:OWNED, :]
    zh, zl = split2(zbuf[...])
    zz = jnp.concatenate([zh, zl], axis=0)
    pair = [jnp.concatenate([pan[0], pan[1]], axis=1), jnp.concatenate([pan[2], pan[3]], axis=1)]
    prod = nt(pair[0], zz[:, 0:256]) + nt(pair[1], zz[:, 256:512])
    update = prod[0:OWNED, 0:128] + prod[0:OWNED, 128:256]
    is_panel = band < 4
    zown = zbuf[:, pl.ds(pl.multiple_of(jnp.minimum(band, 3) * 128, 128), 128)]
    rest = (own - own.astype(bf16).astype(f32)).astype(bf16)
    fix = nt(rest, zown.astype(bf16))
    out_ref[...] = jnp.where(is_panel, -update - fix, own - update)

    @pl.when(x == 0)
    def _():
        for h in range(NCH):
            acopy(h, 0, y_peer).wait_send()
            acopy(h, 1, y_peer).wait_send()

    @pl.when((x == 1) | (x == 3))
    def _():
        for k in range(3):
            fcopy(0, k, y_peer).wait_send()

    for h in range(NCH):
        bcopy(h).wait_send()
        ccopy(h).wait_send()
        dcopy(h).wait_send()
    for k in range(1, ND):
        to = lax.rem(d + k, ND)
        rg(d, d, k, to).wait_send()
        rm(0, d, d, k, to).wait_send()
        rm(1, d, d, k, to).wait_send()
        ag(agg, d, gg_s, gg_r, k, to).wait_send()
        ag(agm, d, gm_s, gm_r, k, to).wait_send()
    for k in range(1, 8):
        blocks(band, lambda q: strip(here, q, gx_s, gx_r, k, c_peer).wait_send())
    blocks(band, lambda q: strip(here, q, gy_s, gy_r, 0, c_peer).wait_send())
    for k in range(1, 8):
        blocks(lax.rem(chip + k, 8) * 2 + c, lambda q: strip(here, q, gy_s, gy_r, k, c_peer).wait_send())


def kernel(v_hbm, pot_hbm, mass_hbm, mat_hbm, conn_hbm, face_hbm, out_ref, v_ref, pot_ref, mass_ref, mat_ref, conn_ref, face_ref, isem, own, wgt, vrecv, recv, pan, pot_row, mass_row, *scratch):
    d = lax.axis_index("domain")
    band = lax.axis_index("band")
    loads = [pltpu.make_async_copy(src, dst, isem.at[k]) for k, (src, dst) in enumerate((
        (face_hbm, face_ref), (pot_hbm, pot_ref), (v_hbm, v_ref), (conn_hbm, conn_ref), (mat_hbm, mat_ref), (mass_hbm, mass_ref)))]
    for load in loads:
        load.start()
    vrecv[...] = jnp.zeros(vrecv.shape, bf16)
    recv[...] = jnp.zeros(recv.shape, bf16)
    for j in range(4):
        pan[j, NCH * CH:ROWS, :] = jnp.zeros((ROWS - NCH * CH, COLS), bf16)
    barrier = pltpu.get_barrier_semaphore()
    for k in range(1, 16):
        pl.semaphore_signal(barrier, inc=1, device_id={"domain": lax.rem(d + k, ND)}, device_id_type=MESHID)
        pl.semaphore_signal(barrier, inc=1, device_id={"band": lax.rem(band + k, 16)}, device_id_type=MESHID)
    for load in loads[:4]:
        load.wait()
    pot_row[...] = pot_ref[...].reshape(1, OWNED)
    n = len(FILTER)
    f = scratch[:n]

    def barrier_wait():
        pl.semaphore_wait(barrier, 30)
        loads[4].wait()
        loads[5].wait()
        mass_row[...] = mass_ref[...].reshape(1, OWNED)

    filter_states(d, barrier_wait, v_ref, pot_row, mass_row, mat_ref, conn_ref, face_ref, own,
                  *f[:22], recv, f[22], vrecv, *f[23:], wgt)
    ortho(own, out_ref, d, band, wgt, pan, *scratch[n:])


V = pltpu.VMEM
D = pltpu.SemaphoreType.DMA
FILTER = (
    V((8, CS), f32), V((8, 256), f32), V((CS, 128), i32), V((256, 128), i32), V((ROWS, 128), f32),
    V((CP, CP), bf16), V((CS, CS), bf16), V((2 * FP, CS), bf16), V((CS, 512), bf16), V((ROWS, CS), bf16),
    V((ROWS, 256), bf16), V((CS, ROWS), bf16), V((ROWS, 512), bf16), V((CS, 128), f32), V((FP, 128), f32),
    V((CS, 128), f32), V((ROWS, 128), f32), V((2, CS, COLS), f32), V((CS, COLS), bf16), V((2, FP, COLS), f32),
    V((CS, COLS), f32),
    V((DEGREE, 2, FP, COLS), bf16), V((FP, COLS), bf16),
    D((DEGREE, 2)), D((DEGREE, 2)), D((2,)),
)
ORTHO = (
    V((320, ROWS), bf16), V((2, 128, 256), f32), V((2, ND, 8, 256), f32), V((128, 128), f32), V((ND, 8, 128), f32),
    V((128, 128), f32), V((128, 512), f32), V((16, 128, 128), f32), V((32, 512), f32), V((512, 512), f32), V((4, 128, 128), f32),
    V((128, 512), f32), V((128, 512), f32), V((ROWS, COLS), f32),
    D((2, NCH)), D((NCH,)), D((NCH,)), D((NCH,)), D((NCH,)), D((NCH,)), D((NCH,)), D((NCH,)), D((3,)),
    D((ND,)), D((ND,)), D((2, ND)), D((2, ND)), D((ND,)), D((ND,)), D((ND,)), D((ND,)), D((8, 4)), D((16, 4)), D((8, 4)), D((16, 4)),
)
SHARED = (V((OWNED, COLS), f32), V((OWNED,), f32), V((OWNED,), f32), V((CELL, CELL), bf16), V((2, CELL), i32), V((1, FACE), i32), D((6,)),
          V((ROWS, COLS), f32), V((ROWS, 128), f32), V((256, COLS), bf16), V((DEGREE, 512, COLS), bf16), V((4, ROWS, COLS), bf16), V((1, OWNED), f32), V((1, OWNED), f32))


def per_device(states, potential, node_mass, cell_matrix, connectivity, face_rows):
    return pl.pallas_call(
        kernel,
        out_shape=jax.ShapeDtypeStruct((OWNED, COLS), f32),
        in_specs=[pl.BlockSpec(memory_space=pltpu.HBM)] * 6,
        out_specs=VM,
        scratch_shapes=list(SHARED + FILTER + ORTHO),
        compiler_params=pltpu.CompilerParams(collective_id=0, has_side_effects=True, vmem_limit_bytes=VLIM),
        name="subspace",
    )(states, potential, node_mass, cell_matrix, connectivity, face_rows)


def solution(mesh):
    return jax.shard_map(
        per_device, mesh=mesh,
        in_specs=(P("domain", "band"), P("domain"), P("domain"), P(), P("domain", None), P("domain", None)),
        out_specs=P("domain", "band"), check_vma=False,
    )
```

```python
import functools
import jax
import jax.numpy as jnp
from jax import lax
from jax.experimental import pallas as pl
from jax.experimental.pallas import tpu as pltpu
from jax.sharding import PartitionSpec as P

f32 = jnp.float32
bf16 = jnp.bfloat16
i32 = jnp.int32
OWNED = 1224
ROWS = 1280
CELL = 729
CP = 768
CS = 1536
FACE = 153
FP = 160
COLS = 128
DEGREE = 6
ND = 16
MESHID = pl.DeviceIdType.MESH
VM = pl.BlockSpec(memory_space=pltpu.VMEM)


def dot(a, b):
    return jnp.dot(a, b, preferred_element_type=f32)


def split2(x):
    hi = x.astype(bf16)
    return hi, (x - hi.astype(f32)).astype(bf16)


def split3(x):
    hi = x.astype(bf16)
    rest = x - hi.astype(f32)
    mid = rest.astype(bf16)
    return hi, mid, (rest - mid.astype(f32)).astype(bf16)


def lanes(shape, base=0):
    return lax.broadcasted_iota(i32, shape, 1) + base


def subs(shape, base=0):
    return lax.broadcasted_iota(i32, shape, 0) + base


def onehot(mask):
    return jnp.where(mask, 1.0, 0.0).astype(bf16)


HIGH = lax.Precision.HIGHEST


def nt(a, b, precision=None):
    return lax.dot_general(a, b, (((1,), (1,)), ((), ())), preferred_element_type=f32, precision=precision)


def nn(a, b):
    return jnp.dot(a, b, preferred_element_type=f32, precision=HIGH)


def chol_inverse(block):
    n, groups = 128, 16
    shape = (8, n)
    lane = lanes(shape)
    sub = subs(shape)

    def spread(x, j):
        return jnp.broadcast_to(x[:, j:j + 1], shape)

    def pick(x, i):
        return jnp.take_along_axis(x, jnp.full(shape, i, i32), axis=0)

    a = [block[8 * k:8 * k + 8, :] for k in range(groups)]
    out = []
    diag = [spread(a[0], q) for q in range(8)]
    below = [spread(a[1], q) for q in range(8)]
    ahead = [spread(a[1], 8 + q) for q in range(8)]
    for g in range(groups):
        j0 = 8 * g
        inside = (lane >= j0) & (lane < j0 + 8)
        s = {(i, k): pick(diag[k], i) for k in range(8) for i in range(k, 8)}
        r = [jnp.where(inside, 0.0, pick(a[g], i)) for i in range(8)]
        near = range(g + 2, min(g + 4, groups))
        side = {t: [spread(a[t], j0 + k) for k in range(8)] for t in near}
        inv, done, mult = [], None, None
        acc = jnp.where(inside, 0.0, a[g + 1]) if g + 1 < groups else None
        for k in range(8):
            root = lax.rsqrt(s[k, k])
            inv.append(root * root)
            r[k] = jnp.where(lane == j0 + k, 1.0, r[k])
            for i in range(k + 1, 8):
                m = s[i, k] * inv[k]
                for q in range(k + 1, i + 1):
                    s[i, q] = s[i, q] - m * s[q, k]
                r[i] = r[i] - m * r[k]
            if g + 1 < groups:
                m = below[k] * inv[k]
                for q in range(8):
                    ahead[q] = ahead[q] - m * pick(below[k], q)
                for q in range(k + 1, 8):
                    below[q] = below[q] - m * s[q, k]
                acc = acc - m * r[k]
            row, part = r[k] * root, r[k] * inv[k]
            done = row if done is None else jnp.where(sub == k, row, done)
            mult = part if mult is None else jnp.where(sub == k, part, mult)
        out.append(jnp.where(lane <= sub + j0, done, 0.0))
        if g + 1 < groups:
            a[g + 1] = acc
        for t in near:
            c = side[t]
            new = jnp.where(inside, 0.0, a[t])
            for k in range(8):
                m = c[k] * inv[k]
                for q in range(k + 1, 8):
                    c[q] = c[q] - m * s[q, k]
                new = new - m * r[k]
            a[t] = new
        if g + 4 < groups:
            t0 = 8 * (g + 4)
            full = None
            for i in range(8):
                full = r[i] if full is None else jnp.where(sub == i, r[i], full)
            far = jnp.dot(mult.T[t0:n, :], full, preferred_element_type=f32, precision=HIGH)
            for t in range(g + 4, groups):
                a[t] = jnp.where(inside, 0.0, a[t]) - far[8 * t - t0:8 * t - t0 + 8, :]
        diag = ahead
        if g + 2 < groups:
            below = [spread(a[g + 2], j0 + 8 + q) for q in range(8)]
            ahead = [spread(a[g + 2], j0 + 16 + q) for q in range(8)]
    return jnp.concatenate(out, axis=0)


def nt3(a, b):
    ah, al = split2(a)
    bh, bl = split2(b)
    return nt(jnp.concatenate([ah, ah, al], axis=1), jnp.concatenate([bh, bl, bh], axis=1))


def nn3(a, b):
    ah, al = split2(a)
    bh, bl = split2(b)
    return dot(jnp.concatenate([ah, ah, al], axis=1), jnp.concatenate([bh, bl, bh], axis=0))


def factor(ext, inv, ybuf, arrive):
    def forward(i):
        a, b = 128 * i, 128 * i + 128
        y = nt3(ybuf[:, a:b], inv[i])
        ybuf[:, a:b] = y
        if i < 3:
            ybuf[:, b:512] = ybuf[:, b:512] - nt3(y, ext[b:512, a:b])

    for i in range(4):
        a, b = 128 * i, 128 * i + 128
        t = chol_inverse(ext[a:b, a:b])
        inv[i] = t
        if i < 3:
            low = nt3(ext[b:512, a:b], t)
            ext[b:512, a:b] = low
            ext[b:512, b:512] = ext[b:512, b:512] - nt3(low, low)
        if i == 1:
            arrive()
            forward(0)
        if i > 0:
            forward(i)


def solve(ext, inv, ybuf, zbuf, band):
    eye = jnp.where(lanes((128, 128)) == subs((128, 128)), 1.0, 0.0)
    for i in (3, 2, 1, 0):
        a, b = 128 * i, 128 * i + 128
        y = jnp.where(band < 4, jnp.where(band == i, -eye, 0.0), ybuf[:, a:b])
        if i < 3:
            y = y - nn3(zbuf[:, b:512], ext[b:512, a:b])
        zbuf[:, a:b] = nn3(y, inv[i])


NCH = 6
VLIM = 60 << 20
CH = 208


def filter_states(d, barrier_wait, v_ref, pot_ref, mass_ref, mat_ref, conn_ref, face_ref, own,
                  crow, frow, connb, faceb, potb, kp, amat, afac, bmat, gt, ft, gsel, v3, potc, potf, msk,
                  cnt, ws, wb, wf, ybuf, send, recv, vsend, vrecv, ssem, rsem, vsem, wgt):
    crow[...] = jnp.full(crow.shape, -1.0, f32)
    crow[0:1, 0:CELL] = conn_ref[0:1, :].astype(f32)
    crow[0:1, CP:CP + CELL] = conn_ref[1:2, :].astype(f32)
    frow[...] = jnp.full(frow.shape, -2.0, f32)
    frow[0:1, 0:FACE] = face_ref[0:1, :].astype(f32)
    for t in range(2):
        row = frow[0:1, 128 * t:128 * t + 128]
        faceb[128 * t:128 * t + 128, :] = jnp.broadcast_to(row, (128, 128)).T.astype(i32)
    potb[1152:1280, :] = jnp.zeros((128, 128), f32)
    v3[1216:ROWS, :] = jnp.zeros((ROWS - 1216, 512), bf16)
    for t in range(9):
        row = pot_ref[0:1, 128 * t:128 * t + 128]
        potb[128 * t:128 * t + 128, :] = jnp.broadcast_to(row, (128, 128)).T
    potb[OWNED - 128:OWNED, :] = jnp.broadcast_to(pot_ref[0:1, OWNED - 128:OWNED], (128, 128)).T
    hi, lo = split2(v_ref[...])
    v3[0:OWNED, 0:128] = hi
    v3[0:OWNED, 128:256] = lo
    hi, lo = split2(potb[0:OWNED, :])
    v3[0:OWNED, 256:384] = hi
    v3[0:OWNED, 384:512] = lo

    fsel = onehot(jnp.tile(faceb[0:FP, :], (1, ROWS // 128)) == lanes((FP, ROWS)))
    fv = dot(fsel, v3[...])
    vface = fv[:, 0:128] + fv[:, 128:256]
    potf[...] = fv[:, 256:384] + fv[:, 384:512]
    wf[0] = vface
    wf[1] = jnp.zeros((FP, COLS), f32)
    vsend[...] = vface.astype(bf16)
    ws[1] = jnp.zeros((CS, COLS), f32)
    barrier_wait()

    def vcopy(dst):
        return pltpu.make_async_remote_copy(
            src_ref=vsend, dst_ref=vrecv.at[pl.ds(0, FP), :], send_sem=vsem.at[0], recv_sem=vsem.at[1],
            device_id={"domain": dst}, device_id_type=MESHID)

    @pl.when(d > 0)
    def _():
        vcopy(d - 1).start()

    for t in range(CS // 128):
        row = crow[0:1, 128 * t:128 * t + 128]
        connb[128 * t:128 * t + 128, :] = jnp.broadcast_to(row, (128, 128)).T.astype(i32)
    kp[...] = jnp.zeros(kp.shape, bf16)
    kp[0:CELL, 0:CELL] = mat_ref[...]
    ci = crow[0:1, :].astype(i32)
    fi = frow[0:1, :].astype(i32)
    tup = onehot(subs((FP, CS), OWNED) == ci)
    tlo = onehot(jnp.tile(faceb[0:FP, :], (1, CS // 128)) == ci)
    both = jnp.concatenate([tup, tlo], axis=0)
    for c in range(2):
        cols = slice(CP * c, CP * c + CP)
        afac[:, cols] = dot(both[:, cols], kp[...]).astype(bf16)
    for t in range(ROWS // 128):
        gsel[:, 128 * t:128 * t + 128] = onehot(connb[...] == lanes((CS, 128), 128 * t))
    cv = dot(gsel[...], v3[:, 0:256])
    ws[0] = cv[:, 0:128] + cv[:, 128:256]
    cb2 = jnp.tile(connb[...], (1, 2))
    bmat[:, 256:512] = onehot(cb2 == lanes((CS, 256), OWNED))

    @pl.when(d < ND - 1)
    def _():
        vcopy(d).wait_recv()

    first = ws[0] + dot(bmat[:, 256:512], vrecv[...])
    ws[0] = first
    wb[...] = first.astype(bf16)

    def up(t, dst):
        return pltpu.make_async_remote_copy(
            src_ref=send.at[t, 0], dst_ref=recv.at[t, pl.ds(0, FP), :], send_sem=ssem.at[t, 0], recv_sem=rsem.at[t, 0],
            device_id={"domain": dst}, device_id_type=MESHID)

    def down(t, dst):
        return pltpu.make_async_remote_copy(
            src_ref=send.at[t, 1], dst_ref=recv.at[t, pl.ds(256, FP), :], send_sem=ssem.at[t, 1], recv_sem=rsem.at[t, 1],
            device_id={"domain": dst}, device_id_type=MESHID)

    def step(t, carry):
        now, then = lax.rem(t, 2), lax.rem(t + 1, 2)
        coef = jnp.where(t == 0, 0.125, 0.25).astype(f32)
        keep = jnp.where(t == 0, 0.0, 1.0).astype(f32)
        x = wb[...]
        send[t, 0] = dot(afac[0:FP, :], x).astype(bf16)

        @pl.when(d < ND - 1)
        def _():
            up(t, d + 1).start()

        wface = wf[now]
        lower = dot(afac[FP:2 * FP, :], x) + potf[...] * wface
        send[t, 1] = lower.astype(bf16)

        @pl.when(d > 0)
        def _():
            down(t, d - 1).start()

        @pl.when(t == 0)
        def _():
            km = kp[...]
            amat[0:CP, 0:CP] = km
            amat[CP:CS, CP:CS] = km
            none = jnp.zeros((CP, CP), bf16)
            c0 = jnp.tile(connb[0:CP, :], (1, CP // 128))
            e01 = jnp.where(c0 >= 0, onehot(c0 == crow[0:1, CP:CS].astype(i32)), none)
            amat[0:CP, CP:CS] = dot(e01, km).astype(bf16)
            c1 = jnp.tile(connb[CP:CS, :], (1, CP // 128))
            e10 = jnp.where(c1 >= 0, onehot(c1 == crow[0:1, 0:CP].astype(i32)), none)
            amat[CP:CS, 0:CP] = dot(e10, km).astype(bf16)
            cp = dot(gsel[...], v3[:, 256:512])
            potc[...] = cp[:, 0:128] + cp[:, 128:256]
            bmat[:, 0:256] = onehot(jnp.tile(connb[...], (1, 2)) == fi)
            msk[...] = jnp.where((connb[...] >= OWNED) & (d == ND - 1), 0.0, 1.0)

        ybuf[...] = coef * (dot(amat[...], x) * msk[...] + (potc[...] - 9.0) * ws[now]) - keep * ws[then]

        @pl.when(t < 5)
        def _():
            at = pl.ds(pl.multiple_of(256 * t, 256), 256)
            g = onehot(subs((256, CS), 256 * t) == ci)
            h = onehot(subs((256, 256), 256 * t) == fi)
            gt[at, :] = g
            ft[at, :] = h
            cnt[at, :] = dot(g, jnp.ones((CS, COLS), bf16)) + dot(h, jnp.ones((256, COLS), bf16))

        @pl.when(t == 5)
        def _():
            for s in range(9):
                row = mass_ref[0:1, 128 * s:128 * s + 128]
                wgt[128 * s:128 * s + 128, :] = jnp.broadcast_to(row, (128, 128)).T * (1.0 / (ND * OWNED))
            wgt[1152:ROWS, :] = jnp.zeros((ROWS - 1152, 128), f32)
            row = mass_ref[0:1, OWNED - 128:OWNED]
            wgt[OWNED - 128:OWNED, :] = jnp.broadcast_to(row, (128, 128)).T * (1.0 / (ND * OWNED))

        @pl.when(d > 0)
        def _():
            up(t, d).wait_recv()

        @pl.when(d < ND - 1)
        def _():
            down(t, d).wait_recv()

        got = recv[t]
        wf[then] = coef * (lower + got[0:FP].astype(f32) - 9.0 * wface) - keep * wf[then]
        new = ybuf[...] + coef * dot(bmat[...], got)
        ws[then] = new
        wb[...] = new.astype(bf16)
        return carry

    lax.fori_loop(0, DEGREE, step, 0)

    @pl.when(d > 0)
    def _():
        vcopy(d).wait_send()
        for t in range(DEGREE):
            down(t, d).wait_send()

    @pl.when(d < ND - 1)
    def _():
        for t in range(DEGREE):
            up(t, d).wait_send()

    hi, lo = split2(ws[DEGREE % 2])
    back = dot(gt[...], jnp.concatenate([hi, lo], axis=1))
    hi, lo = split2(wf[DEGREE % 2])
    pad = jnp.zeros((256 - FP, 256), bf16)
    fback = dot(ft[...], jnp.concatenate([jnp.concatenate([hi, lo], axis=1), pad], axis=0))
    summed = (back + fback)[0:OWNED]
    count = cnt[0:OWNED, :]
    x = (potb[0:OWNED, :] - 9.0) * 0.125
    x2 = x * x
    alone = ((32.0 * x2 - 48.0) * x2 + 18.0) * x2 - 1.0
    own[0:OWNED, :] = jnp.where(count > 0.5, (summed[:, 0:128] + summed[:, 128:256]) / jnp.maximum(count, 1.0), alone * v_ref[...])
    own[OWNED:ROWS, :] = jnp.zeros((ROWS - OWNED, COLS), f32)


def strip_of(band):
    x = band // 4
    return 4 * (2 * lax.rem(band // 2, 2) + x // 2) + lax.rem(x, 2) * 2 + lax.rem(band, 2)


def ortho(own_ref, out_ref, d, band, wgt, pan, wt, sbm, rsm, sbg, rsg, agg, agm, gbuf, stripbuf, ext, inv, ybuf, zbuf, wcol,
          asem_s, asem_r, bsem_s, bsem_r, csem_s, csem_r, dsem_s, dsem_r, fsem_s,
          rg_s, rg_r, rm_s, rm_r, gg_s, gg_r, gm_s, gm_r, gx_s, gx_r, gy_s, gy_r):
    x = band // 4
    yh = lax.rem(band // 2, 2)
    c = lax.rem(band, 2)
    mine = lax.rem(band, 4)

    def copy(src, dst, ss, rs, to):
        return pltpu.make_async_remote_copy(src_ref=src, dst_ref=dst, send_sem=ss, recv_sem=rs,
                                            device_id={"band": to}, device_id_type=MESHID)

    def part(block, h):
        return pan.at[block, pl.ds(pl.multiple_of(h * CH, 16), CH), :]

    def acopy(h, slot, to):
        return copy(part(mine, h), part(mine, h), asem_s.at[slot, h], asem_r.at[h], to)

    y_peer = x * 4 + (1 - yh) * 2 + c
    c_peer = x * 4 + yh * 2 + (1 - c)
    across = (1 - yh) * 2 + c

    @pl.when(x == 0)
    def _():
        pan[mine, 0:NCH * CH, :] = own_ref[0:NCH * CH, :].astype(bf16)
        for k in range(NCH):
            acopy(k, 0, band + 4).start()
            acopy((k + 3) % NCH, 1, band + 12).start()

    def order(k):
        return jnp.where(x == 3, (k + 3) % NCH, jnp.where(x == 2, (k % 2) * 3 + k // 2, k))

    def bcopy(h):
        return copy(part(mine, h), part(mine, h), bsem_s.at[h], bsem_r.at[h], y_peer)

    def ccopy(h):
        return copy(part(mine, h), part(mine, h), csem_s.at[h], csem_r.at[h], c_peer)

    def dcopy(h):
        return copy(part(across, h), part(across, h), dsem_s.at[h], dsem_r.at[h], c_peer)

    def fcopy(h, k, to):
        return copy(part(mine, h), part(mine, h), fsem_s.at[k], asem_r.at[h], to)

    for k in range(NCH):
        h = order(k)

        @pl.when(x > 0)
        def _():
            acopy(h, 0, band).wait_recv()

        if k < 3:
            @pl.when((x == 1) | (x == 3))
            def _():
                fcopy(h, k, mine + 8).start()
        bcopy(h).start()
        ccopy(h).start()

    for t in range(10):
        at = slice(128 * t, 128 * t + 128)
        hi, lo = split2((own_ref[at, :] * wgt[at, :]).T)
        wt[0:128, at] = hi
        wt[128:256, at] = lo

    for h in range(NCH):
        copy(part(mine, h), part(mine, h), csem_s.at[h], csem_r.at[h], c_peer).wait_recv()
    wcol[...] = pan[2 * yh + x // 2].astype(f32) * wgt[...]
    sub = pl.multiple_of((lax.rem(x, 2) * 2 + c) * 32, 32)
    for t in range(10):
        at = slice(128 * t, 128 * t + 128)
        ybuf[0:128, 0:128] = wcol[at, :].T
        hi, lo = split2(ybuf[pl.ds(sub, 32), 0:128])
        wt[256:288, at] = hi
        wt[288:320, at] = lo

    def rows(m):
        return pl.ds(pl.multiple_of(m * 8, 8), 8)

    def rm(p, src_rows, slot, ss, to):
        return pltpu.make_async_remote_copy(
            src_ref=sbm.at[p, rows(src_rows), :], dst_ref=rsm.at[p, slot], send_sem=rm_s.at[p, ss], recv_sem=rm_r.at[p, slot],
            device_id={"domain": to}, device_id_type=MESHID)

    def rg(src_rows, slot, ss, to):
        return pltpu.make_async_remote_copy(
            src_ref=sbg.at[rows(src_rows), :], dst_ref=rsg.at[slot], send_sem=rg_s.at[ss], recv_sem=rg_r.at[slot],
            device_id={"domain": to}, device_id_type=MESHID)

    def products(p, panel):
        both = jnp.concatenate([pan[2 * panel], pan[2 * panel + 1]], axis=1)
        r = dot(wt[...], both)
        sbm[p] = r[0:128] + r[128:256]
        stripbuf[:, pl.ds(pl.multiple_of(panel * 256, 256), 256)] = r[256:288] + r[288:320]

    products(0, yh)
    for k in range(1, ND):
        to = lax.rem(d + k, ND)
        rm(0, to, d, k, to).start()

    for k in range(NCH):
        h = order(k)
        copy(part(across, h), part(across, h), bsem_s.at[h], bsem_r.at[h], y_peer).wait_recv()
        dcopy(h).start()
    for h in range(NCH):
        copy(part(mine, h), part(mine, h), dsem_s.at[h], dsem_r.at[h], c_peer).wait_recv()

    products(1, 1 - yh)
    for m in range(ND):
        sbg[8 * m:8 * m + 8, :] = stripbuf[8 * (m % 4):8 * (m % 4) + 8, 128 * (m // 4):128 * (m // 4) + 128]
    for k in range(1, ND):
        to = lax.rem(d + k, ND)
        rg(to, d, k, to).start()
    for k in range(1, ND):
        to = lax.rem(d + k, ND)
        rm(1, to, d, k, to).start()
    rsg[d] = sbg[rows(d), :]
    rsm[0, d] = sbm[0, rows(d), :]
    rsm[1, d] = sbm[1, rows(d), :]
    for k in range(1, ND):
        frm = lax.rem(d + k, ND)
        rg(frm, frm, k, frm).wait_recv()
    total = rsg[0]
    for m in range(1, ND):
        total = total + rsg[m]
    agg[rows(d), :] = total

    def ag(buf, who, ss, rr, k, to):
        view = buf.at[rows(who), :]
        return pltpu.make_async_remote_copy(
            src_ref=view, dst_ref=view, send_sem=ss.at[k], recv_sem=rr.at[who],
            device_id={"domain": to}, device_id_type=MESHID)

    for k in range(1, ND):
        to = lax.rem(d + k, ND)
        ag(agg, d, gg_s, gg_r, k, to).start()
    for k in range(1, ND):
        frm = lax.rem(d + k, ND)
        ag(agg, frm, gg_s, gg_r, k, frm).wait_recv()

    here = strip_of(band)
    gbuf[here] = agg[...]
    chip = band // 2

    def row_of(b):
        return 2 * lax.rem(b // 2, 2) + b // 8

    def strip(who, q, ss, rr, k, to):
        view = gbuf.at[who, pl.ds(32 * q, 32), :]
        return copy(view, view, ss.at[k, q], rr.at[who, q], to)

    def blocks(b, act):
        for q in range(4):
            if q == 3:
                act(q)
            else:
                pl.when(row_of(b) <= q)(functools.partial(act, q))

    for k in range(1, 8):
        to = lax.rem(chip + k, 8) * 2 + c
        blocks(band, lambda q: strip(here, q, gx_s, gx_r, k, to).start())
    blocks(band, lambda q: strip(here, q, gy_s, gy_r, 0, c_peer).start())
    for p in range(2):
        for k in range(1, ND):
            frm = lax.rem(d + k, ND)
            rm(p, frm, frm, k, frm).wait_recv()
        total = rsm[p, 0]
        for m in range(1, ND):
            total = total + rsm[p, m]
        panel = yh if p == 0 else 1 - yh
        agm[rows(d), pl.ds(pl.multiple_of(panel * 256, 256), 256)] = total
    for k in range(1, ND):
        to = lax.rem(d + k, ND)
        ag(agm, d, gm_s, gm_r, k, to).start()
    for k in range(1, 8):
        who = lax.rem(chip + k, 8) * 2 + c
        frm = strip_of(who)

        def relay(q):
            strip(frm, q, gx_s, gx_r, k, c_peer).wait_recv()
            strip(frm, q, gy_s, gy_r, k, c_peer).start()

        blocks(who, relay)
    for k in range(8):
        who = lax.rem(chip + k, 8) * 2 + (1 - c)
        frm = strip_of(who)
        blocks(who, lambda q: strip(frm, q, gy_s, gy_r, k, c_peer).wait_recv())

    for b in range(16):
        for m in range(ND):
            if m // 4 >= b // 4:
                ext[32 * b + 8 * (m % 4):32 * b + 8 * (m % 4) + 8, 128 * (m // 4):128 * (m // 4) + 128] = gbuf[b, 8 * m:8 * m + 8, :]
    for i in range(3):
        for j in range(i + 1, 4):
            ext[128 * j:128 * j + 128, 128 * i:128 * i + 128] = ext[128 * i:128 * i + 128, 128 * j:128 * j + 128].T

    def arrive():
        for k in range(1, ND):
            frm = lax.rem(d + k, ND)
            ag(agm, frm, gm_s, gm_r, k, frm).wait_recv()
        ybuf[...] = agm[...]

    factor(ext, inv, ybuf, arrive)
    solve(ext, inv, ybuf, zbuf, band)

    own = own_ref[0:OWNED, :]
    zh, zl = split2(zbuf[...])
    zz = jnp.concatenate([zh, zl], axis=0)
    pair = [jnp.concatenate([pan[0], pan[1]], axis=1), jnp.concatenate([pan[2], pan[3]], axis=1)]
    prod = nt(pair[0], zz[:, 0:256]) + nt(pair[1], zz[:, 256:512])
    update = prod[0:OWNED, 0:128] + prod[0:OWNED, 128:256]
    is_panel = band < 4
    zown = zbuf[:, pl.ds(pl.multiple_of(jnp.minimum(band, 3) * 128, 128), 128)]
    rest = (own - own.astype(bf16).astype(f32)).astype(bf16)
    fix = nt(rest, zown.astype(bf16))
    out_ref[...] = jnp.where(is_panel, -update - fix, own - update)

    @pl.when(x == 0)
    def _():
        for h in range(NCH):
            acopy(h, 0, y_peer).wait_send()
            acopy(h, 1, y_peer).wait_send()

    @pl.when((x == 1) | (x == 3))
    def _():
        for k in range(3):
            fcopy(0, k, y_peer).wait_send()

    for h in range(NCH):
        bcopy(h).wait_send()
        ccopy(h).wait_send()
        dcopy(h).wait_send()
    for k in range(1, ND):
        to = lax.rem(d + k, ND)
        rg(d, d, k, to).wait_send()
        rm(0, d, d, k, to).wait_send()
        rm(1, d, d, k, to).wait_send()
        ag(agg, d, gg_s, gg_r, k, to).wait_send()
        ag(agm, d, gm_s, gm_r, k, to).wait_send()
    for k in range(1, 8):
        blocks(band, lambda q: strip(here, q, gx_s, gx_r, k, c_peer).wait_send())
    blocks(band, lambda q: strip(here, q, gy_s, gy_r, 0, c_peer).wait_send())
    for k in range(1, 8):
        blocks(lax.rem(chip + k, 8) * 2 + c, lambda q: strip(here, q, gy_s, gy_r, k, c_peer).wait_send())


def kernel(v_hbm, pot_hbm, mass_hbm, mat_hbm, conn_hbm, face_hbm, out_ref, v_ref, pot_ref, mass_ref, mat_ref, conn_ref, face_ref, isem, own, wgt, vrecv, recv, pan, pot_row, mass_row, *scratch):
    d = lax.axis_index("domain")
    band = lax.axis_index("band")
    loads = [pltpu.make_async_copy(src, dst, isem.at[k]) for k, (src, dst) in enumerate((
        (face_hbm, face_ref), (pot_hbm, pot_ref), (v_hbm, v_ref), (conn_hbm, conn_ref), (mat_hbm, mat_ref), (mass_hbm, mass_ref)))]
    for load in loads:
        load.start()
    vrecv[...] = jnp.zeros(vrecv.shape, bf16)
    recv[...] = jnp.zeros(recv.shape, bf16)
    for j in range(4):
        pan[j, NCH * CH:ROWS, :] = jnp.zeros((ROWS - NCH * CH, COLS), bf16)
    barrier = pltpu.get_barrier_semaphore()
    for k in range(1, 16):
        pl.semaphore_signal(barrier, inc=1, device_id={"domain": lax.rem(d + k, ND)}, device_id_type=MESHID)
        pl.semaphore_signal(barrier, inc=1, device_id={"band": lax.rem(band + k, 16)}, device_id_type=MESHID)
    for load in loads[:4]:
        load.wait()
    pot_row[...] = pot_ref[...].reshape(1, OWNED)
    n = len(FILTER)
    f = scratch[:n]

    def barrier_wait():
        pl.semaphore_wait(barrier, 30)
        loads[4].wait()
        loads[5].wait()
        mass_row[...] = mass_ref[...].reshape(1, OWNED)

    filter_states(d, barrier_wait, v_ref, pot_row, mass_row, mat_ref, conn_ref, face_ref, own,
                  *f[:22], recv, f[22], vrecv, *f[23:], wgt)
    ortho(own, out_ref, d, band, wgt, pan, *scratch[n:])


V = pltpu.VMEM
D = pltpu.SemaphoreType.DMA
FILTER = (
    V((8, CS), f32), V((8, 256), f32), V((CS, 128), i32), V((256, 128), i32), V((ROWS, 128), f32),
    V((CP, CP), bf16), V((CS, CS), bf16), V((2 * FP, CS), bf16), V((CS, 512), bf16), V((ROWS, CS), bf16),
    V((ROWS, 256), bf16), V((CS, ROWS), bf16), V((ROWS, 512), bf16), V((CS, 128), f32), V((FP, 128), f32),
    V((CS, 128), f32), V((ROWS, 128), f32), V((2, CS, COLS), f32), V((CS, COLS), bf16), V((2, FP, COLS), f32),
    V((CS, COLS), f32),
    V((DEGREE, 2, FP, COLS), bf16), V((FP, COLS), bf16),
    D((DEGREE, 2)), D((DEGREE, 2)), D((2,)),
)
ORTHO = (
    V((320, ROWS), bf16), V((2, 128, 256), f32), V((2, ND, 8, 256), f32), V((128, 128), f32), V((ND, 8, 128), f32),
    V((128, 128), f32), V((128, 512), f32), V((16, 128, 128), f32), V((32, 512), f32), V((512, 512), f32), V((4, 128, 128), f32),
    V((128, 512), f32), V((128, 512), f32), V((ROWS, COLS), f32),
    D((2, NCH)), D((NCH,)), D((NCH,)), D((NCH,)), D((NCH,)), D((NCH,)), D((NCH,)), D((NCH,)), D((3,)),
    D((ND,)), D((ND,)), D((2, ND)), D((2, ND)), D((ND,)), D((ND,)), D((ND,)), D((ND,)), D((8, 4)), D((16, 4)), D((8, 4)), D((16, 4)),
)
SHARED = (V((OWNED, COLS), f32), V((OWNED,), f32), V((OWNED,), f32), V((CELL, CELL), bf16), V((2, CELL), i32), V((1, FACE), i32), D((6,)),
          V((ROWS, COLS), f32), V((ROWS, 128), f32), V((256, COLS), bf16), V((DEGREE, 512, COLS), bf16), V((4, ROWS, COLS), bf16), V((1, OWNED), f32), V((1, OWNED), f32))


def per_device(states, potential, node_mass, cell_matrix, connectivity, face_rows):
    return pl.pallas_call(
        kernel,
        out_shape=jax.ShapeDtypeStruct((OWNED, COLS), f32),
        in_specs=[pl.BlockSpec(memory_space=pltpu.HBM)] * 6,
        out_specs=VM,
        scratch_shapes=list(SHARED + FILTER + ORTHO),
        compiler_params=pltpu.CompilerParams(collective_id=0, has_side_effects=True, vmem_limit_bytes=VLIM),
        name="subspace",
    )(states, potential, node_mass, cell_matrix, connectivity, face_rows)


def solution(mesh):
    return jax.shard_map(
        per_device, mesh=mesh,
        in_specs=(P("domain", "band"), P("domain"), P("domain"), P(), P("domain", None), P("domain", None)),
        out_specs=P("domain", "band"), check_vma=False,
    )
```
